128 devices in a mesh: tm: 16 (over x, y), rows: 8 (over z, core).
Axes of the slice: x: 4, y: 4, z: 4, core: 2. Of those that a mesh axis runs over, the one named last changes fastest.
Arguments:
- features: bfloat16 [64, 128, 48, 256], P('tm', 'rows'), may hold values from -16 to 16
- gamma_one: float32 [256], replicated, may hold values from 0.1 to 1.9
- beta_one: float32 [256], replicated, may hold values from -3 to 3
- weight_one: bfloat16 [3, 3, 3, 256, 256], replicated, may hold values from -0.078125 to 0.078125
- bias_one: float32 [256], replicated, may hold values from -3 to 3
- gamma_two: float32 [256], replicated, may hold values from 0.1 to 1.9
- beta_two: float32 [256], replicated, may hold values from -3 to 3
- weight_two: bfloat16 [3, 3, 3, 256, 256], replicated, may hold values from -0.078125 to 0.078125
- bias_two: float32 [256], replicated, may hold values from -3 to 3
Outputs:
- block_out: bfloat16 [64, 128, 48, 256], P('tm', 'rows')
The draws below stay inside these ranges and needn't reach their ends.
All inputs are finite; a program needn't handle non-finite values.
Results may differ from the reference program's by a relative error of at most 0.006.
Values may be sent and summed in bfloat16 or wider, within the bound.
A program may use at most 128 MiB of HBM per device.

```python
import math
import jax
import jax.numpy as jnp
from jax import lax

C = 256
GROUPS = 32
COLS = 48
TFRAMES = 64
HEIGHT = 128


def draw_features(key, part):
    keys = jax.random.split(key, 4)
    spread = math.log(10.0) / 2.0
    cell_scale = jnp.exp(jax.random.uniform(keys[0], (1, HEIGHT, COLS, 1), jnp.float32, -spread, spread))
    chan_scale = jnp.exp(jax.random.uniform(keys[1], (1, 1, 1, C), jnp.float32, -spread, spread))
    jitter = jnp.exp(jax.random.uniform(keys[2], (TFRAMES, 1, 1, 1), jnp.float32, math.log(0.7), math.log(1.4)))
    trend = jnp.exp(math.log(3.0) * jnp.arange(TFRAMES, dtype=jnp.float32) / max(TFRAMES - 1, 1)).reshape(TFRAMES, 1, 1, 1)
    base = jax.random.normal(keys[3], (TFRAMES, HEIGHT, COLS, C), jnp.float32)
    values = 0.5 * base * cell_scale * chan_scale * jitter * trend
    return jnp.clip(values, -16.0, 16.0).astype(jnp.bfloat16)


def noise(key, shape, scale, reach, held_as=jnp.bfloat16):
    array = scale * jax.random.normal(key, shape, jnp.float32)
    return jnp.clip(array, min=-reach, max=reach).astype(held_as)


def setup_inputs(seed: int = 0) -> dict:
    seeds = jax.random.split(jax.random.key(seed), 10)
    features = draw_features(jax.random.fold_in(seeds[9], 71), 0)
    gamma_one = jnp.clip(1.0 + 0.18 * jax.random.normal(seeds[1], (C,), jnp.float32), 0.1, 1.9)
    beta_one = noise(seeds[2], (C,), 0.5, 3.0, jnp.float32)
    weight_one = noise(seeds[3], (3, 3, 3, C, C), (27 * C) ** -0.5, 0.078125)
    bias_one = noise(seeds[4], (C,), 0.5, 3.0, jnp.float32)
    gamma_two = jnp.clip(1.0 + 0.18 * jax.random.normal(seeds[5], (C,), jnp.float32), 0.1, 1.9)
    beta_two = noise(seeds[6], (C,), 0.5, 3.0, jnp.float32)
    weight_two = noise(seeds[7], (3, 3, 3, C, C), (27 * C) ** -0.5, 0.078125)
    bias_two = noise(seeds[8], (C,), 0.5, 3.0, jnp.float32)
    return {"features": features, "gamma_one": gamma_one, "beta_one": beta_one, "weight_one": weight_one, "bias_one": bias_one, "gamma_two": gamma_two, "beta_two": beta_two, "weight_two": weight_two, "bias_two": bias_two}


epsilon = 1e-06

def causal_norm(widened, gain, shift):
    frame_count, row_count, col_count, chan_count = widened.shape
    per_group = chan_count // GROUPS
    first_sum = lax.optimization_barrier(jnp.sum(widened, axis=(1, 2))).reshape(frame_count, GROUPS, per_group).sum(-1)
    square_sum = lax.optimization_barrier(jnp.sum(widened * widened, axis=(1, 2))).reshape(frame_count, GROUPS, per_group).sum(-1)
    running_one = jnp.cumsum(first_sum, axis=0)
    running_two = jnp.cumsum(square_sum, axis=0)
    entries = ((jnp.arange(frame_count, dtype=jnp.float32) + 1.0) * float(row_count * col_count * per_group))[:, None]
    group_mean = running_one / entries
    group_var = running_two / entries - group_mean * group_mean
    inv_std = lax.rsqrt(group_var + epsilon)
    mean_chan = jnp.repeat(group_mean, per_group, axis=1)[:, None, None, :]
    scale_chan = jnp.repeat(inv_std, per_group, axis=1)[:, None, None, :]
    normed = (widened - mean_chan) * scale_chan * gain + shift
    return jax.nn.silu(normed).astype(jnp.bfloat16)

def causal_conv(activated, weight, bias):
    frame_count, row_count, col_count, chan_count = activated.shape
    padded = jnp.pad(activated, ((2, 0), (1, 1), (1, 1), (0, 0)))
    matrices = weight.reshape(3, 9 * chan_count, chan_count)

    def one_frame(frame):
        window = lax.dynamic_slice_in_dim(padded, frame, 3, 0)
        total = jnp.zeros((row_count * col_count, chan_count), jnp.float32)
        for tap_row in range(3):
            pieces = [window[tap_time, tap_row:tap_row + row_count, tap_col:tap_col + col_count, :] for tap_time in range(3) for tap_col in range(3)]
            slab = jnp.concatenate(pieces, axis=-1).reshape(row_count * col_count, 9 * chan_count)
            total = total + jnp.dot(slab, matrices[tap_row], preferred_element_type=jnp.float32)
        return total.reshape(row_count, col_count, chan_count)
    result = lax.map(one_frame, jnp.arange(frame_count, dtype=jnp.int32))
    return result + bias

def reference(features, gamma_one, beta_one, weight_one, bias_one, gamma_two, beta_two, weight_two, bias_two):
    widened = features.astype(jnp.float32)
    first = causal_norm(widened, gamma_one, beta_one)
    between = causal_conv(first, weight_one, bias_one).astype(jnp.bfloat16)
    second = causal_norm(between.astype(jnp.float32), gamma_two, beta_two)
    return (causal_conv(second, weight_two, bias_two) + widened).astype(jnp.bfloat16)
```

```python
import functools

import jax
import jax.numpy as jnp
from jax import lax
from jax.experimental import pallas as pl
from jax.experimental.pallas import tpu as pltpu
from jax.sharding import PartitionSpec as P

MESH = pl.DeviceIdType.MESH
GROUPS = 32
EPSILON = 1e-06
HBM = pl.BlockSpec(memory_space=pltpu.HBM)


def group_sum(x, per_group):
    lane = lax.broadcasted_iota(jnp.int32, x.shape, 1)
    step = 1
    while step < per_group:
        up = pltpu.roll(x, x.shape[1] - step, 1)
        down = pltpu.roll(x, step, 1)
        x = x + jnp.where((lane & step) == 0, up, down)
        step *= 2
    return x


def block_kernel(n_tm, n_rw, frames, rows, cols, chans,
                 feat, g1, b1, w1, c1, g2, b2, w2, c2, out,
                 fx, bx, xn, wa, wb, ob, par, sl, ra, tb, st,
                 lsem, psem, wsem, osem, rsend, rrecv, tsend, trecv, hsend, hrecv):
    tm = lax.axis_index("tm")
    rw = lax.axis_index("rows")
    pix = rows * cols
    per_group = chans // GROUPS

    loads = [pltpu.make_async_copy(feat.at[f], fx.at[2 + f, 1:rows + 1], lsem.at[f]) for f in range(frames)]
    for c in loads:
        c.start()
    small = [pltpu.make_async_copy(p, par.at[i], psem.at[i]) for i, p in enumerate((g1, b1, c1, g2, b2, c2))]
    for c in small:
        c.start()
    taps = [
        pltpu.make_async_copy(w.at[:, e], v.at[:, :, e * chans:(e + 1) * chans], wsem.at[n, e])
        for n, (w, v) in enumerate(((w1, wa), (w2, wb))) for e in range(3)
    ]
    for c in taps:
        c.start()

    tb[...] = jnp.zeros_like(tb)

    barrier = pltpu.get_barrier_semaphore()
    for k in range(1, n_rw):
        pl.semaphore_signal(barrier, 1, device_id=(tm, lax.rem(rw + k, n_rw)), device_id_type=MESH)
    for k in range(1, n_tm):
        pl.semaphore_signal(barrier, 1, device_id=(lax.rem(tm + k, n_tm), rw), device_id_type=MESH)
    for dt in (-1, 1):
        for dr in (-1, 1):
            @pl.when((tm + dt >= 0) & (tm + dt < n_tm) & (rw + dr >= 0) & (rw + dr < n_rw))
            def _():
                pl.semaphore_signal(barrier, 1, device_id=(tm + dt, rw + dr), device_id_type=MESH)

    def frame_sums(z):
        part1 = jnp.sum(z.reshape(z.shape[0] // 8, 8, chans), axis=0)
        part2 = jnp.sum((z * z).reshape(z.shape[0] // 8, 8, chans), axis=0)
        return part1, part2

    def put_sums(which, f, part1, part2):
        sl[which, pl.ds(f, 1), :] = jnp.sum(part1, axis=0, keepdims=True)
        sl[which, pl.ds(frames + f, 1), :] = jnp.sum(part2, axis=0, keepdims=True)

    for f in range(frames):
        loads[f].wait()

        def add_row(r, carry, f=f):
            one, two = frame_sums(fx[2 + f, 1 + r].astype(jnp.float32))
            return carry[0] + one, carry[1] + two

        zero = jnp.zeros((8, chans), jnp.float32)
        one, two = lax.fori_loop(0, rows, add_row, (zero, zero))
        put_sums(0, f, one, two)

    n_diag = (jnp.where(tm > 0, 1, 0) + jnp.where(tm < n_tm - 1, 1, 0)) * (
        jnp.where(rw > 0, 1, 0) + jnp.where(rw < n_rw - 1, 1, 0))
    pl.semaphore_wait(barrier, n_rw - 1 + n_tm - 1 + n_diag)

    def halo(buf, n, kind, e):
        def remote(src, dst, dev):
            return pltpu.make_async_remote_copy(
                src_ref=src, dst_ref=dst, send_sem=hsend.at[n, kind, e], recv_sem=hrecv.at[n, kind, e],
                device_id=dev, device_id_type=MESH)
        if kind == 0:
            return remote(buf.at[e, rows], buf.at[e, 0], (tm, rw + 1))
        if kind == 1:
            return remote(buf.at[e, 1], buf.at[e, rows + 1], (tm, rw - 1))
        if kind == 2:
            return remote(buf.at[e + frames, 1:rows + 1], buf.at[e, 1:rows + 1], (tm + 1, rw))
        if kind == 3:
            return remote(buf.at[e + frames, rows], buf.at[e, 0], (tm + 1, rw + 1))
        return remote(buf.at[e + frames, 1], buf.at[e, rows + 1], (tm + 1, rw - 1))

    sends = (rw < n_rw - 1, rw > 0, tm < n_tm - 1,
             (tm < n_tm - 1) & (rw < n_rw - 1), (tm < n_tm - 1) & (rw > 0))
    gets = (rw > 0, rw < n_rw - 1, tm > 0, (tm > 0) & (rw > 0), (tm > 0) & (rw < n_rw - 1))

    def halo_start(buf, n, kinds, e):
        for kind in kinds:
            @pl.when(sends[kind])
            def _():
                halo(buf, n, kind, e).start()

    def halo_sent(buf, n, kinds, e):
        for kind in kinds:
            @pl.when(sends[kind])
            def _():
                halo(buf, n, kind, e).wait_send()

    def halo_here(buf, n, kinds, e):
        for kind in kinds:
            @pl.when(gets[kind])
            def _():
                halo(buf, n, kind, e).wait_recv()

    def row_copy(n, k):
        return pltpu.make_async_remote_copy(
            src_ref=sl.at[n], dst_ref=ra.at[n, k - 1], send_sem=rsend.at[n, k - 1], recv_sem=rrecv.at[n, k - 1],
            device_id=(tm, lax.rem(rw + k, n_rw)), device_id_type=MESH)

    def time_copy(n, k):
        return pltpu.make_async_remote_copy(
            src_ref=sl.at[2 + n], dst_ref=tb.at[n, k - 1], send_sem=tsend.at[n, k - 1], recv_sem=trecv.at[n, k - 1],
            device_id=(tm + k, rw), device_id_type=MESH)

    def stats_start(n):
        for k in (4, 5, 3, 2, 6, 7, 1):
            row_copy(n, k).start()

    def stats_finish(n, gain, shift):
        for k in range(1, n_rw):
            row_copy(n, k).wait_recv()
        mine = sl[n] + jnp.sum(ra[n], axis=0)
        sl[2 + n] = mine
        for k in (10, 6, 9, 11, 14, 2, 5, 7, 8, 12, 13, 15, 3, 4, 1):
            @pl.when(tm + k < n_tm)
            def _():
                time_copy(n, k).start()
        for k in range(1, n_tm):
            @pl.when(tm >= k)
            def _():
                time_copy(n, k).wait_recv()
        far = jnp.sum(tb[n, 1:], axis=0)
        near = tb[n, 0]

        def running(lo):
            total = jnp.sum(far[lo:lo + frames], axis=0, keepdims=True)
            for f in range(frames - 1):
                total = total + near[lo + f:lo + f + 1]
            result = [total]
            total = total + near[lo + frames - 1:lo + frames]
            result.append(total)
            for f in range(frames):
                total = total + mine[lo + f:lo + f + 1]
                result.append(total)
            pad = jnp.zeros((8 - len(result), chans), jnp.float32)
            return group_sum(jnp.concatenate(result + [pad], axis=0), per_group)

        one, two = running(0), running(frames)
        place = lax.broadcasted_iota(jnp.int32, one.shape, 0)
        count = jnp.maximum(tm * frames + place - 1, 1).astype(jnp.float32) * float(n_rw * pix * per_group)
        mean = one / count
        var = two / count - mean * mean
        st[0] = mean
        st[1] = lax.rsqrt(var + EPSILON) * (0.5 * gain)
        st[2, 0:1] = 0.5 * shift

    def stats_sent(n):
        for k in range(1, n_rw):
            row_copy(n, k).wait_send()
        for k in range(1, n_tm):
            @pl.when(tm + k < n_tm)
            def _():
                time_copy(n, k).wait_send()

    def normalise(buf, e):
        mean, scale, shift = st[0, pl.ds(e, 1), :], st[1, pl.ds(e, 1), :], st[2, 0:1]

        def one(r):
            half = (buf[e, r].astype(jnp.float32) - mean) * scale + shift
            xn[e, pl.ds(pl.multiple_of(r * cols, cols), cols), :] = (half + half * jnp.tanh(half)).astype(jnp.bfloat16)

        def nothing(r):
            xn[e, pl.ds(r * cols, cols), :] = jnp.zeros((cols, chans), jnp.bfloat16)

        there = (tm > 0) | (e >= 2)

        @pl.when(there)
        def _():
            def two(i, _):
                one(1 + 2 * i)
                one(2 + 2 * i)
                return 0
            lax.fori_loop(0, rows // 2, two, 0)

        @pl.when(there & (rw > 0))
        def _():
            one(0)

        @pl.when(there & (rw < n_rw - 1))
        def _():
            one(rows + 1)

        @pl.when(jnp.logical_not(there))
        def _():
            xn[e] = jnp.zeros_like(xn[e])

        @pl.when(there & (rw == 0))
        def _():
            nothing(0)

        @pl.when(there & (rw == n_rw - 1))
        def _():
            nothing(rows + 1)

    col = lax.broadcasted_iota(jnp.int32, (pix, chans), 0) % cols

    def conv(w, f):
        total = None
        for a in range(3):
            for t in range(3):
                part = jnp.dot(xn[f + t, a * cols:a * cols + pix, :], w[a * 3 + t],
                               preferred_element_type=jnp.float32)
                total = part if total is None else total + part
        left = jnp.where(col == 0, 0.0, pltpu.roll(total[:, :chans], 1, 0))
        right = jnp.where(col == cols - 1, 0.0, pltpu.roll(total[:, 2 * chans:], pix - 1, 0))
        return total[:, chans:2 * chans] + left + right

    stats_start(0)
    for e in (1, 0):
        halo_start(fx, 0, (2, 3, 4), e)
    for e in range(2, 2 + frames):
        halo_start(fx, 0, (0, 1), e)
    for c in small:
        c.wait()
    stats_finish(0, par[0], par[1])
    for e in range(2, 2 + frames):
        halo_here(fx, 0, (0, 1), e)
        normalise(fx, e)
    for c in taps[:3]:
        c.wait()

    def first_conv(i, _):
        f = frames - 1 - i

        @pl.when(f < 2)
        def _():
            halo_here(fx, 0, (2, 3, 4), f)
            normalise(fx, f)

        y = (conv(wa, f) + par[2]).astype(jnp.bfloat16)
        bx[2 + f, 1:rows + 1] = y.reshape(rows, cols, chans)
        put_sums(1, f, *frame_sums(y.astype(jnp.float32)))
        halo_start(bx, 1, (0, 1), 2 + f)

        @pl.when(f >= frames - 2)
        def _():
            halo_start(bx, 1, (2, 3, 4), f + 2 - frames)
        return 0

    lax.fori_loop(0, frames, first_conv, 0)

    stats_start(1)
    stats_finish(1, par[3], par[4])
    for e in range(2, 2 + frames):
        halo_here(bx, 1, (0, 1), e)
        normalise(bx, e)
    for c in taps[3:]:
        c.wait()

    def out_copy(f):
        return pltpu.make_async_copy(ob.at[f], out.at[f], osem.at[f])

    def second_conv(i, _):
        f = frames - 1 - i

        @pl.when(f < 2)
        def _():
            halo_here(bx, 1, (2, 3, 4), f)
            normalise(bx, f)

        y = conv(wb, f) + par[5] + fx[2 + f, 1:rows + 1].reshape(pix, chans).astype(jnp.float32)
        ob[f] = y.astype(jnp.bfloat16).reshape(rows, cols, chans)
        out_copy(f).start()
        return 0

    lax.fori_loop(0, frames, second_conv, 0)

    for f in range(frames):
        out_copy(f).wait()
    for n, buf in enumerate((fx, bx)):
        for e in (1, 0):
            halo_sent(buf, n, (2, 3, 4), e)
        for e in range(2, 2 + frames):
            halo_sent(buf, n, (0, 1), e)
        stats_sent(n)


def solution(mesh):
    n_tm, n_rw = mesh.shape["tm"], mesh.shape["rows"]

    def on_device(features, gamma_one, beta_one, weight_one, bias_one, gamma_two, beta_two, weight_two, bias_two):
        frames, rows, cols, chans = features.shape
        taps = lambda w: w.reshape(9, 3, chans, chans)
        line = lambda v: v.reshape(1, chans)
        bf16, f32 = jnp.bfloat16, jnp.float32
        dma = pltpu.SemaphoreType.DMA
        return pl.pallas_call(
            functools.partial(block_kernel, n_tm, n_rw, frames, rows, cols, chans),
            out_shape=jax.ShapeDtypeStruct(features.shape, bf16),
            in_specs=[HBM] * 9,
            out_specs=HBM,
            scratch_shapes=[
                pltpu.VMEM((frames + 2, rows + 2, cols, chans), bf16),
                pltpu.VMEM((frames + 2, rows + 2, cols, chans), bf16),
                pltpu.VMEM((frames + 2, (rows + 2) * cols, chans), bf16),
                pltpu.VMEM((9, chans, 3 * chans), bf16),
                pltpu.VMEM((9, chans, 3 * chans), bf16),
                pltpu.VMEM(features.shape, bf16),
                pltpu.VMEM((6, 1, chans), f32),
                pltpu.VMEM((4, 2 * frames, chans), f32),
                pltpu.VMEM((2, n_rw - 1, 2 * frames, chans), f32),
                pltpu.VMEM((2, n_tm - 1, 2 * frames, chans), f32),
                pltpu.VMEM((3, 8, chans), f32),
                dma((frames,)), dma((6,)), dma((2, 3)), dma((frames,)),
                dma((2, n_rw - 1)), dma((2, n_rw - 1)), dma((2, n_tm - 1)), dma((2, n_tm - 1)),
                dma((2, 5, frames + 2)), dma((2, 5, frames + 2)),
            ],
            compiler_params=pltpu.CompilerParams(
                collective_id=0, has_side_effects=True, vmem_limit_bytes=48 << 20),
        )(features, line(gamma_one), line(beta_one), taps(weight_one), line(bias_one),
          line(gamma_two), line(beta_two), taps(weight_two), line(bias_two))

    placed = (P("tm", "rows", None, None), P(), P(), P(), P(), P(), P(), P(), P())
    return jax.shard_map(on_device, mesh=mesh, in_specs=placed, out_specs=P("tm", "rows", None, None), check_vma=False)
```

```python
import functools

import jax
import jax.numpy as jnp
from jax import lax
from jax.experimental import pallas as pl
from jax.experimental.pallas import tpu as pltpu
from jax.sharding import PartitionSpec as P

MESH = pl.DeviceIdType.MESH
GROUPS = 32
EPSILON = 1e-06
HBM = pl.BlockSpec(memory_space=pltpu.HBM)


def group_sum(x, per_group):
    lane = lax.broadcasted_iota(jnp.int32, x.shape, 1)
    step = 1
    while step < per_group:
        up = pltpu.roll(x, x.shape[1] - step, 1)
        down = pltpu.roll(x, step, 1)
        x = x + jnp.where((lane & step) == 0, up, down)
        step *= 2
    return x


def block_kernel(n_tm, n_rw, frames, rows, cols, chans,
                 feat, g1, b1, w1, c1, g2, b2, w2, c2, out,
                 fx, bx, xn, wa, wb, ob, par, sl, ra, tb, st,
                 lsem, psem, wsem, osem, rsend, rrecv, tsend, trecv, hsend, hrecv):
    tm = lax.axis_index("tm")
    rw = lax.axis_index("rows")
    pix = rows * cols
    per_group = chans // GROUPS

    loads = [pltpu.make_async_copy(feat.at[f], fx.at[2 + f, 1:rows + 1], lsem.at[f]) for f in range(frames)]
    for c in loads:
        c.start()
    small = [pltpu.make_async_copy(p, par.at[i], psem.at[i]) for i, p in enumerate((g1, b1, c1, g2, b2, c2))]
    for c in small:
        c.start()
    taps = [
        pltpu.make_async_copy(w.at[:, e], v.at[:, :, e * chans:(e + 1) * chans], wsem.at[n, e])
        for n, (w, v) in enumerate(((w1, wa), (w2, wb))) for e in range(3)
    ]
    for c in taps:
        c.start()

    tb[...] = jnp.zeros_like(tb)

    barrier = pltpu.get_barrier_semaphore()
    for k in range(1, n_rw):
        pl.semaphore_signal(barrier, 1, device_id=(tm, lax.rem(rw + k, n_rw)), device_id_type=MESH)
    for k in range(1, n_tm):
        pl.semaphore_signal(barrier, 1, device_id=(lax.rem(tm + k, n_tm), rw), device_id_type=MESH)
    for dt in (-1, 1):
        for dr in (-1, 1):
            @pl.when((tm + dt >= 0) & (tm + dt < n_tm) & (rw + dr >= 0) & (rw + dr < n_rw))
            def _():
                pl.semaphore_signal(barrier, 1, device_id=(tm + dt, rw + dr), device_id_type=MESH)

    def frame_sums(z):
        part1 = jnp.sum(z.reshape(z.shape[0] // 8, 8, chans), axis=0)
        part2 = jnp.sum((z * z).reshape(z.shape[0] // 8, 8, chans), axis=0)
        return part1, part2

    def put_sums(which, f, part1, part2):
        sl[which, pl.ds(f, 1), :] = jnp.sum(part1, axis=0, keepdims=True)
        sl[which, pl.ds(frames + f, 1), :] = jnp.sum(part2, axis=0, keepdims=True)

    for f in range(frames):
        loads[f].wait()

        def add_row(r, carry, f=f):
            one, two = frame_sums(fx[2 + f, 1 + r].astype(jnp.float32))
            return carry[0] + one, carry[1] + two

        zero = jnp.zeros((8, chans), jnp.float32)
        one, two = lax.fori_loop(0, rows, add_row, (zero, zero))
        put_sums(0, f, one, two)

    n_diag = (jnp.where(tm > 0, 1, 0) + jnp.where(tm < n_tm - 1, 1, 0)) * (
        jnp.where(rw > 0, 1, 0) + jnp.where(rw < n_rw - 1, 1, 0))
    pl.semaphore_wait(barrier, n_rw - 1 + n_tm - 1 + n_diag)

    quarter = rows // 4

    def halo(buf, n, kind, e):
        def remote(src, dst, dev):
            return pltpu.make_async_remote_copy(
                src_ref=src, dst_ref=dst, send_sem=hsend.at[n, kind, e], recv_sem=hrecv.at[n, kind, e],
                device_id=dev, device_id_type=MESH)
        if kind == 0:
            return remote(buf.at[e, rows], buf.at[e, 0], (tm, rw + 1))
        if kind == 1:
            return remote(buf.at[e, 1], buf.at[e, rows + 1], (tm, rw - 1))
        if kind == 2:
            return remote(buf.at[e + frames, rows], buf.at[e, 0], (tm + 1, rw + 1))
        if kind == 3:
            return remote(buf.at[e + frames, 1], buf.at[e, rows + 1], (tm + 1, rw - 1))
        part = pl.ds(1 + (kind - 4) * quarter, quarter)
        return remote(buf.at[e + frames, part], buf.at[e, part], (tm + 1, rw))

    ROW, TIME = (0, 1), (2, 3, 4, 5, 6, 7)
    sends = (rw < n_rw - 1, rw > 0, (tm < n_tm - 1) & (rw < n_rw - 1), (tm < n_tm - 1) & (rw > 0)) + (tm < n_tm - 1,) * 4
    gets = (rw > 0, rw < n_rw - 1, (tm > 0) & (rw > 0), (tm > 0) & (rw < n_rw - 1)) + (tm > 0,) * 4

    def halo_start(buf, n, kinds, e):
        for kind in kinds:
            @pl.when(sends[kind])
            def _():
                halo(buf, n, kind, e).start()

    def halo_sent(buf, n, kinds, e):
        for kind in kinds:
            @pl.when(sends[kind])
            def _():
                halo(buf, n, kind, e).wait_send()

    def halo_here(buf, n, kinds, e):
        for kind in kinds:
            @pl.when(gets[kind])
            def _():
                halo(buf, n, kind, e).wait_recv()

    def row_copy(n, k):
        return pltpu.make_async_remote_copy(
            src_ref=sl.at[n], dst_ref=ra.at[n, k - 1], send_sem=rsend.at[n, k - 1], recv_sem=rrecv.at[n, k - 1],
            device_id=(tm, lax.rem(rw + k, n_rw)), device_id_type=MESH)

    def time_copy(n, k):
        return pltpu.make_async_remote_copy(
            src_ref=sl.at[2 + n], dst_ref=tb.at[n, k - 1], send_sem=tsend.at[n, k - 1], recv_sem=trecv.at[n, k - 1],
            device_id=(tm + k, rw), device_id_type=MESH)

    def stats_start(n):
        for k in (4, 5, 3, 2, 6, 7, 1):
            row_copy(n, k).start()

    def stats_finish(n, gain, shift, rest):
        for k in range(1, n_rw):
            row_copy(n, k).wait_recv()
        mine = sl[n] + jnp.sum(ra[n], axis=0)
        sl[2 + n] = mine
        for k in (10, 6, 9, 11, 14, 2, 5, 7, 8, 12, 13, 15, 3, 4, 1):
            @pl.when(tm + k < n_tm)
            def _():
                time_copy(n, k).start()
        rest()
        for k in range(1, n_tm):
            @pl.when(tm >= k)
            def _():
                time_copy(n, k).wait_recv()
        far = jnp.sum(tb[n, 1:], axis=0)
        near = tb[n, 0]

        def running(lo):
            total = jnp.sum(far[lo:lo + frames], axis=0, keepdims=True)
            for f in range(frames - 1):
                total = total + near[lo + f:lo + f + 1]
            result = [total]
            total = total + near[lo + frames - 1:lo + frames]
            result.append(total)
            for f in range(frames):
                total = total + mine[lo + f:lo + f + 1]
                result.append(total)
            pad = jnp.zeros((8 - len(result), chans), jnp.float32)
            return group_sum(jnp.concatenate(result + [pad], axis=0), per_group)

        one, two = running(0), running(frames)
        place = lax.broadcasted_iota(jnp.int32, one.shape, 0)
        count = jnp.maximum(tm * frames + place - 1, 1).astype(jnp.float32) * float(n_rw * pix * per_group)
        mean = one / count
        var = two / count - mean * mean
        st[0] = mean
        st[1] = lax.rsqrt(var + EPSILON) * (0.5 * gain)
        st[2, 0:1] = 0.5 * shift

    def stats_sent(n):
        for k in range(1, n_rw):
            row_copy(n, k).wait_send()
        for k in range(1, n_tm):
            @pl.when(tm + k < n_tm)
            def _():
                time_copy(n, k).wait_send()

    def normalise(buf, e):
        mean, scale, shift = st[0, pl.ds(e, 1), :], st[1, pl.ds(e, 1), :], st[2, 0:1]

        def one(r):
            half = (buf[e, r].astype(jnp.float32) - mean) * scale + shift
            xn[e, pl.ds(pl.multiple_of(r * cols, cols), cols), :] = (half + half * jnp.tanh(half)).astype(jnp.bfloat16)

        def nothing(r):
            xn[e, pl.ds(r * cols, cols), :] = jnp.zeros((cols, chans), jnp.bfloat16)

        there = (tm > 0) | (e >= 2)

        @pl.when(there)
        def _():
            def two(i, _):
                one(1 + 2 * i)
                one(2 + 2 * i)
                return 0
            lax.fori_loop(0, rows // 2, two, 0)

        @pl.when(there & (rw > 0))
        def _():
            one(0)

        @pl.when(there & (rw < n_rw - 1))
        def _():
            one(rows + 1)

        @pl.when(jnp.logical_not(there))
        def _():
            xn[e] = jnp.zeros_like(xn[e])

        @pl.when(there & (rw == 0))
        def _():
            nothing(0)

        @pl.when(there & (rw == n_rw - 1))
        def _():
            nothing(rows + 1)

    col = lax.broadcasted_iota(jnp.int32, (pix, chans), 0) % cols

    def conv(w, f):
        total = None
        for a in range(3):
            for t in range(3):
                part = jnp.dot(xn[f + t, a * cols:a * cols + pix, :], w[a * 3 + t],
                               preferred_element_type=jnp.float32)
                total = part if total is None else total + part
        left = jnp.where(col == 0, 0.0, pltpu.roll(total[:, :chans], 1, 0))
        right = jnp.where(col == cols - 1, 0.0, pltpu.roll(total[:, 2 * chans:], pix - 1, 0))
        return total[:, chans:2 * chans] + left + right

    stats_start(0)
    for e in range(2, 2 + frames):
        halo_start(fx, 0, ROW, e)
    halo_start(fx, 0, (4,), 1)

    def rest_first():
        halo_start(fx, 0, (5, 6, 7, 2, 3), 1)
        halo_start(fx, 0, TIME, 0)

    for c in small:
        c.wait()
    stats_finish(0, par[0], par[1], rest_first)
    for e in range(2, 2 + frames):
        halo_here(fx, 0, ROW, e)
        normalise(fx, e)
    for c in taps[:3]:
        c.wait()

    def first_conv(i, _):
        f = frames - 1 - i

        @pl.when(f < 2)
        def _():
            halo_here(fx, 0, TIME, f)
            normalise(fx, f)

        y = (conv(wa, f) + par[2]).astype(jnp.bfloat16)
        bx[2 + f, 1:rows + 1] = y.reshape(rows, cols, chans)
        put_sums(1, f, *frame_sums(y.astype(jnp.float32)))
        halo_start(bx, 1, ROW, 2 + f)

        @pl.when(i == 1)
        def _():
            halo_start(bx, 1, (4,), 1)

        @pl.when(i == 2)
        def _():
            halo_start(bx, 1, (5,), 1)
        return 0

    lax.fori_loop(0, frames, first_conv, 0)

    def rest_second():
        halo_start(bx, 1, (7, 2, 3), 1)
        halo_start(bx, 1, TIME, 0)

    stats_start(1)
    halo_start(bx, 1, (6,), 1)
    stats_finish(1, par[3], par[4], rest_second)
    for e in range(2, 2 + frames):
        halo_here(bx, 1, ROW, e)
        normalise(bx, e)
    for c in taps[3:]:
        c.wait()

    def out_copy(f):
        return pltpu.make_async_copy(ob.at[f], out.at[f], osem.at[f])

    def second_conv(i, _):
        f = frames - 1 - i

        @pl.when(f < 2)
        def _():
            halo_here(bx, 1, TIME, f)
            normalise(bx, f)

        y = conv(wb, f) + par[5] + fx[2 + f, 1:rows + 1].reshape(pix, chans).astype(jnp.float32)
        ob[f] = y.astype(jnp.bfloat16).reshape(rows, cols, chans)
        out_copy(f).start()
        return 0

    lax.fori_loop(0, frames, second_conv, 0)

    for f in range(frames):
        out_copy(f).wait()
    for n, buf in enumerate((fx, bx)):
        for e in (1, 0):
            halo_sent(buf, n, TIME, e)
        for e in range(2, 2 + frames):
            halo_sent(buf, n, ROW, e)
        stats_sent(n)


def solution(mesh):
    n_tm, n_rw = mesh.shape["tm"], mesh.shape["rows"]

    def on_device(features, gamma_one, beta_one, weight_one, bias_one, gamma_two, beta_two, weight_two, bias_two):
        frames, rows, cols, chans = features.shape
        taps = lambda w: w.reshape(9, 3, chans, chans)
        line = lambda v: v.reshape(1, chans)
        bf16, f32 = jnp.bfloat16, jnp.float32
        dma = pltpu.SemaphoreType.DMA
        return pl.pallas_call(
            functools.partial(block_kernel, n_tm, n_rw, frames, rows, cols, chans),
            out_shape=jax.ShapeDtypeStruct(features.shape, bf16),
            in_specs=[HBM] * 9,
            out_specs=HBM,
            scratch_shapes=[
                pltpu.VMEM((frames + 2, rows + 2, cols, chans), bf16),
                pltpu.VMEM((frames + 2, rows + 2, cols, chans), bf16),
                pltpu.VMEM((frames + 2, (rows + 2) * cols, chans), bf16),
                pltpu.VMEM((9, chans, 3 * chans), bf16),
                pltpu.VMEM((9, chans, 3 * chans), bf16),
                pltpu.VMEM(features.shape, bf16),
                pltpu.VMEM((6, 1, chans), f32),
                pltpu.VMEM((4, 2 * frames, chans), f32),
                pltpu.VMEM((2, n_rw - 1, 2 * frames, chans), f32),
                pltpu.VMEM((2, n_tm - 1, 2 * frames, chans), f32),
                pltpu.VMEM((3, 8, chans), f32),
                dma((frames,)), dma((6,)), dma((2, 3)), dma((frames,)),
                dma((2, n_rw - 1)), dma((2, n_rw - 1)), dma((2, n_tm - 1)), dma((2, n_tm - 1)),
                dma((2, 8, frames + 2)), dma((2, 8, frames + 2)),
            ],
            compiler_params=pltpu.CompilerParams(
                collective_id=0, has_side_effects=True, vmem_limit_bytes=64000 << 10),
        )(features, line(gamma_one), line(beta_one), taps(weight_one), line(bias_one),
          line(gamma_two), line(beta_two), taps(weight_two), line(bias_two))

    placed = (P("tm", "rows", None, None), P(), P(), P(), P(), P(), P(), P(), P())
    return jax.shard_map(on_device, mesh=mesh, in_specs=placed, out_specs=P("tm", "rows", None, None), check_vma=False)
```

```python
import functools

import jax
import jax.numpy as jnp
from jax import lax
from jax.experimental import pallas as pl
from jax.experimental.pallas import tpu as pltpu
from jax.sharding import PartitionSpec as P

MESH = pl.DeviceIdType.MESH
GROUPS = 32
EPSILON = 1e-06
HBM = pl.BlockSpec(memory_space=pltpu.HBM)


def group_sum(x, per_group):
    lane = lax.broadcasted_iota(jnp.int32, x.shape, 1)
    step = 1
    while step < per_group:
        up = pltpu.roll(x, x.shape[1] - step, 1)
        down = pltpu.roll(x, step, 1)
        x = x + jnp.where((lane & step) == 0, up, down)
        step *= 2
    return x


def block_kernel(n_tm, n_rw, frames, rows, cols, chans,
                 feat, g1, b1, w1, c1, g2, b2, w2, c2, out,
                 fx, bx, xn, un, wa, wb, va, vb, par, sl, ra, tb, st,
                 lsem, psem, wsem, rsend, rrecv, tsend, trecv, hsend, hrecv):
    tm = lax.axis_index("tm")
    rw = lax.axis_index("rows")
    pix = rows * cols
    per_group = chans // GROUPS

    loads = [pltpu.make_async_copy(feat.at[f], fx.at[2 + f, 1:rows + 1], lsem.at[f]) for f in range(frames)]
    for c in loads:
        c.start()
    small = [pltpu.make_async_copy(p, par.at[i], psem.at[i]) for i, p in enumerate((g1, b1, c1, g2, b2, c2))]
    for c in small:
        c.start()
    taps = [
        pltpu.make_async_copy(w.at[:, e], v.at[:, :, e * chans:(e + 1) * chans], wsem.at[n, e])
        for n, (w, v) in enumerate(((w1, wa), (w2, wb))) for e in range(3)
    ]
    for c in taps:
        c.start()

    tb[...] = jnp.zeros_like(tb)

    barrier = pltpu.get_barrier_semaphore()
    for k in range(1, n_rw):
        pl.semaphore_signal(barrier, 1, device_id=(tm, lax.rem(rw + k, n_rw)), device_id_type=MESH)
    for k in range(1, n_tm):
        pl.semaphore_signal(barrier, 1, device_id=(lax.rem(tm + k, n_tm), rw), device_id_type=MESH)

    def frame_sums(z):
        part1 = jnp.sum(z.reshape(z.shape[0] // 8, 8, chans), axis=0)
        part2 = jnp.sum((z * z).reshape(z.shape[0] // 8, 8, chans), axis=0)
        return part1, part2

    def put_sums(which, f, part1, part2):
        sl[which, pl.ds(f, 1), :] = jnp.sum(part1, axis=0, keepdims=True)
        sl[which, pl.ds(frames + f, 1), :] = jnp.sum(part2, axis=0, keepdims=True)

    for f in range(frames):
        loads[f].wait()

        def add_row(r, carry, f=f):
            one, two = frame_sums(fx[2 + f, 1 + r].astype(jnp.float32))
            return carry[0] + one, carry[1] + two

        zero = jnp.zeros((8, chans), jnp.float32)
        one, two = lax.fori_loop(0, rows, add_row, (zero, zero))
        put_sums(0, f, one, two)

    pl.semaphore_wait(barrier, n_rw - 1 + n_tm - 1)

    quarter = rows // 4

    def halo(buf, n, kind, e):
        def remote(src, dst, dev):
            return pltpu.make_async_remote_copy(
                src_ref=src, dst_ref=dst, send_sem=hsend.at[n, kind, e], recv_sem=hrecv.at[n, kind, e],
                device_id=dev, device_id_type=MESH)
        if kind == 0:
            return remote(buf.at[e, rows], buf.at[e, 0], (tm, rw + 1))
        if kind == 1:
            return remote(buf.at[e, 1], buf.at[e, rows + 1], (tm, rw - 1))
        part = pl.ds(1 + (kind - 2) * quarter, quarter)
        return remote(buf.at[e + frames, part], buf.at[e, part], (tm + 1, rw))

    ROW, TIME, EDGES, MIDDLE = (0, 1), (2, 3, 4, 5), (2, 5), (3, 4)
    sends = ((rw < n_rw - 1), (rw > 0)) + (tm < n_tm - 1,) * 4
    gets = ((rw > 0), (rw < n_rw - 1)) + (tm > 0,) * 4

    def halo_start(buf, n, kinds, e):
        for kind in kinds:
            @pl.when(sends[kind])
            def _():
                halo(buf, n, kind, e).start()

    def halo_sent(buf, n, kinds, e):
        for kind in kinds:
            @pl.when(sends[kind])
            def _():
                halo(buf, n, kind, e).wait_send()

    def halo_here(buf, n, kinds, e):
        for kind in kinds:
            @pl.when(gets[kind])
            def _():
                halo(buf, n, kind, e).wait_recv()

    def halo_edge(buf, n, e):
        @pl.when(tm > 0)
        def _():
            halo_start(buf, n, ROW, e)

    def halo_corner(buf, n, e):
        @pl.when(tm > 0)
        def _():
            halo_here(buf, n, ROW, e)

    def row_copy(n, k):
        return pltpu.make_async_remote_copy(
            src_ref=sl.at[n], dst_ref=ra.at[n, k - 1], send_sem=rsend.at[n, k - 1], recv_sem=rrecv.at[n, k - 1],
            device_id=(tm, lax.rem(rw + k, n_rw)), device_id_type=MESH)

    def time_copy(n, k):
        return pltpu.make_async_remote_copy(
            src_ref=sl.at[2 + n], dst_ref=tb.at[n, k - 1], send_sem=tsend.at[n, k - 1], recv_sem=trecv.at[n, k - 1],
            device_id=(tm + k, rw), device_id_type=MESH)

    def stats_start(n):
        for k in (4, 5, 3, 2, 6, 7, 1):
            row_copy(n, k).start()

    def stats_finish(n, gain, shift, rest):
        for k in range(1, n_rw):
            row_copy(n, k).wait_recv()
        mine = sl[n] + jnp.sum(ra[n], axis=0)
        sl[2 + n] = mine
        for k in (10, 6, 9, 11, 14, 2, 5, 7, 8, 12, 13, 15, 3, 4, 1):
            @pl.when(tm + k < n_tm)
            def _():
                time_copy(n, k).start()
        rest()
        for k in range(1, n_tm):
            @pl.when(tm >= k)
            def _():
                time_copy(n, k).wait_recv()
        far = jnp.sum(tb[n, 1:], axis=0)
        near = tb[n, 0]

        def running(lo):
            total = jnp.sum(far[lo:lo + frames], axis=0, keepdims=True)
            for f in range(frames - 1):
                total = total + near[lo + f:lo + f + 1]
            result = [total]
            total = total + near[lo + frames - 1:lo + frames]
            result.append(total)
            for f in range(frames):
                total = total + mine[lo + f:lo + f + 1]
                result.append(total)
            pad = jnp.zeros((8 - len(result), chans), jnp.float32)
            return group_sum(jnp.concatenate(result + [pad], axis=0), per_group)

        one, two = running(0), running(frames)
        place = lax.broadcasted_iota(jnp.int32, one.shape, 0)
        count = jnp.maximum(tm * frames + place - 1, 1).astype(jnp.float32) * float(n_rw * pix * per_group)
        mean = one / count
        var = two / count - mean * mean
        st[0] = mean
        st[1] = lax.rsqrt(var + EPSILON) * (0.5 * gain)
        st[2, 0:1] = 0.5 * shift

    def stats_sent(n):
        for k in range(1, n_rw):
            row_copy(n, k).wait_send()
        for k in range(1, n_tm):
            @pl.when(tm + k < n_tm)
            def _():
                time_copy(n, k).wait_send()

    def normalise(buf, e):
        mean, scale, shift = st[0, pl.ds(e, 1), :], st[1, pl.ds(e, 1), :], st[2, 0:1]

        def one(r):
            half = (buf[e, r].astype(jnp.float32) - mean) * scale + shift
            xn[e, pl.ds(pl.multiple_of(r * cols, cols), cols), :] = (half + half * jnp.tanh(half)).astype(jnp.bfloat16)

        def nothing(r):
            xn[e, pl.ds(r * cols, cols), :] = jnp.zeros((cols, chans), jnp.bfloat16)

        there = (tm > 0) | (e >= 2)

        @pl.when(there)
        def _():
            def two(i, _):
                one(1 + 2 * i)
                one(2 + 2 * i)
                return 0
            lax.fori_loop(0, rows // 2, two, 0)

        @pl.when(there & (rw > 0))
        def _():
            one(0)

        @pl.when(there & (rw < n_rw - 1))
        def _():
            one(rows + 1)

        @pl.when(jnp.logical_not(there))
        def _():
            xn[e] = jnp.zeros_like(xn[e])

        @pl.when(there & (rw == 0))
        def _():
            nothing(0)

        @pl.when(there & (rw == n_rw - 1))
        def _():
            nothing(rows + 1)

    def time_taps(w, v):
        for a in range(3):
            outer = (w[a * 3].astype(jnp.float32) + w[a * 3 + 2].astype(jnp.float32)) * 0.5
            inner = w[a * 3 + 1].astype(jnp.float32) * 0.5
            v[a] = (outer - inner).astype(jnp.bfloat16)
            w[a * 3 + 1] = (outer + inner).astype(jnp.bfloat16)

    def time_frames(f):
        d0, d1, d2, d3 = [xn[f + i].astype(jnp.float32) for i in range(4)]
        un[0] = (d0 - d2).astype(jnp.bfloat16)
        un[1] = (d1 + d2).astype(jnp.bfloat16)
        un[2] = (d2 - d1).astype(jnp.bfloat16)
        un[3] = (d1 - d3).astype(jnp.bfloat16)

    col = lax.broadcasted_iota(jnp.int32, (pix, chans), 0) % cols

    def conv(w, v, bias):
        outs = [None, None]
        for e in (1, 0, 2):
            m = []
            for k in range(4):
                total = None
                for a in range(3):
                    tap = (w.at[a * 3], w.at[a * 3 + 1], v.at[a], w.at[a * 3 + 2])[k]
                    part = jnp.dot(un[k, a * cols:a * cols + pix, :], tap[:, e * chans:(e + 1) * chans],
                                   preferred_element_type=jnp.float32)
                    total = part if total is None else total + part
                m.append(total)
            pair = (m[0] + m[1] + m[2], m[1] - m[2] - m[3])
            for i, y in enumerate(pair):
                if e == 0:
                    y = jnp.where(col == 0, 0.0, pltpu.roll(y, 1, 0))
                if e == 2:
                    y = jnp.where(col == cols - 1, 0.0, pltpu.roll(y, pix - 1, 0))
                outs[i] = y + bias if outs[i] is None else outs[i] + y
        return outs

    stats_start(0)
    for e in range(2, 2 + frames):
        halo_start(fx, 0, ROW, e)
    halo_start(fx, 0, EDGES[:1], 1)
    for c in small:
        c.wait()
    for c in taps[:3]:
        c.wait()
    time_taps(wa, va)

    def rest_first():
        halo_start(fx, 0, EDGES[1:], 1)
        halo_start(fx, 0, EDGES, 0)
        halo_start(fx, 0, MIDDLE, 1)
        halo_start(fx, 0, MIDDLE, 0)
        for c in taps[3:]:
            c.wait()
        time_taps(wb, vb)

    def edges_on(buf, n):
        for e in (1, 0):
            halo_here(buf, n, EDGES, e)
            halo_edge(buf, n, e)

    stats_finish(0, par[0], par[1], rest_first)
    for e in range(2, 2 + frames):
        halo_here(fx, 0, ROW, e)
        normalise(fx, e)

    def first_conv(i, _):
        f = 2 - 2 * i

        @pl.when(i == 1)
        def _():
            edges_on(fx, 0)
            for e in (1, 0):
                halo_here(fx, 0, MIDDLE, e)
                halo_corner(fx, 0, e)
                normalise(fx, e)

        time_frames(f)
        for o, y in enumerate(conv(wa, va, par[2])):
            y = y.astype(jnp.bfloat16)
            bx[2 + f + o, 1:rows + 1] = y.reshape(rows, cols, chans)
            put_sums(1, f + o, *frame_sums(y.astype(jnp.float32)))

        @pl.when(i == 0)
        def _():
            for e in (4, 5):
                halo_start(bx, 1, ROW, e)
            halo_start(bx, 1, EDGES, 1)
        return 0

    lax.fori_loop(0, 2, first_conv, 0)

    def rest_second():
        halo_start(bx, 1, EDGES[1:], 0)
        halo_start(bx, 1, MIDDLE, 1)
        halo_start(bx, 1, MIDDLE, 0)

    stats_start(1)
    for e in (2, 3):
        halo_start(bx, 1, ROW, e)
    halo_start(bx, 1, EDGES[:1], 0)
    stats_finish(1, par[3], par[4], rest_second)
    for e in range(2, 2 + frames):
        halo_here(bx, 1, ROW, e)
        normalise(bx, e)

    def second_conv(i, _):
        f = 2 - 2 * i

        @pl.when(i == 1)
        def _():
            edges_on(bx, 1)
            for e in (1, 0):
                halo_here(bx, 1, MIDDLE, e)
                halo_corner(bx, 1, e)
                normalise(bx, e)

        time_frames(f)
        for o, y in enumerate(conv(wb, vb, par[5])):
            y = y + fx[2 + f + o, 1:rows + 1].reshape(pix, chans).astype(jnp.float32)
            out[f + o] = y.astype(jnp.bfloat16).reshape(rows, cols, chans)
        return 0

    lax.fori_loop(0, 2, second_conv, 0)

    for n, buf in enumerate((fx, bx)):
        for e in (1, 0):
            halo_sent(buf, n, TIME, e)

            @pl.when(tm > 0)
            def _():
                halo_sent(buf, n, ROW, e)
        for e in range(2, 2 + frames):
            halo_sent(buf, n, ROW, e)
        stats_sent(n)


def solution(mesh):
    n_tm, n_rw = mesh.shape["tm"], mesh.shape["rows"]

    def on_device(features, gamma_one, beta_one, weight_one, bias_one, gamma_two, beta_two, weight_two, bias_two):
        frames, rows, cols, chans = features.shape
        taps = lambda w: w.reshape(9, 3, chans, chans)
        line = lambda v: v.reshape(1, chans)
        bf16, f32 = jnp.bfloat16, jnp.float32
        dma = pltpu.SemaphoreType.DMA
        return pl.pallas_call(
            functools.partial(block_kernel, n_tm, n_rw, frames, rows, cols, chans),
            out_shape=jax.ShapeDtypeStruct(features.shape, bf16),
            in_specs=[HBM] * 9,
            out_specs=pl.BlockSpec(memory_space=pltpu.VMEM),
            scratch_shapes=[
                pltpu.VMEM((frames + 2, rows + 2, cols, chans), bf16),
                pltpu.VMEM((frames + 2, rows + 2, cols, chans), bf16),
                pltpu.VMEM((frames + 2, (rows + 2) * cols, chans), bf16),
                pltpu.VMEM((4, (rows + 2) * cols, chans), bf16),
                pltpu.VMEM((9, chans, 3 * chans), bf16),
                pltpu.VMEM((9, chans, 3 * chans), bf16),
                pltpu.VMEM((3, chans, 3 * chans), bf16),
                pltpu.VMEM((3, chans, 3 * chans), bf16),
                pltpu.VMEM((6, 1, chans), f32),
                pltpu.VMEM((4, 2 * frames, chans), f32),
                pltpu.VMEM((2, n_rw - 1, 2 * frames, chans), f32),
                pltpu.VMEM((2, n_tm - 1, 2 * frames, chans), f32),
                pltpu.VMEM((3, 8, chans), f32),
                dma((frames,)), dma((6,)), dma((2, 3)),
                dma((2, n_rw - 1)), dma((2, n_rw - 1)), dma((2, n_tm - 1)), dma((2, n_tm - 1)),
                dma((2, 6, frames + 2)), dma((2, 6, frames + 2)),
            ],
            compiler_params=pltpu.CompilerParams(
                collective_id=0, has_side_effects=True, vmem_limit_bytes=52 << 20),
        )(*[pltpu.with_memory_space_constraint(v, pltpu.HBM) for v in (
            features, line(gamma_one), line(beta_one), taps(weight_one), line(bias_one),
            line(gamma_two), line(beta_two), taps(weight_two), line(bias_two))])

    placed = (P("tm", "rows", None, None), P(), P(), P(), P(), P(), P(), P(), P())
    return jax.shard_map(on_device, mesh=mesh, in_specs=placed, out_specs=P("tm", "rows", None, None), check_vma=False)
```

```python
import functools

import jax
import jax.numpy as jnp
from jax import lax
from jax.experimental import pallas as pl
from jax.experimental.pallas import tpu as pltpu
from jax.sharding import PartitionSpec as P

MESH = pl.DeviceIdType.MESH
GROUPS = 32
EPSILON = 1e-06
HBM = pl.BlockSpec(memory_space=pltpu.HBM)


def group_sum(x, per_group):
    lane = lax.broadcasted_iota(jnp.int32, x.shape, 1)
    step = 1
    while step < per_group:
        up = pltpu.roll(x, x.shape[1] - step, 1)
        down = pltpu.roll(x, step, 1)
        x = x + jnp.where((lane & step) == 0, up, down)
        step *= 2
    return x


def block_kernel(n_tm, n_rw, frames, rows, cols, chans,
                 feat, g1, b1, w1, c1, g2, b2, w2, c2, out,
                 fx, bx, xn, un, acc, wa, wb, va, vb, par, sl, ln, ra, tb, st,
                 lsem, psem, wsem, rsend, rrecv, tsend, trecv, hsend, hrecv):
    tm = lax.axis_index("tm")
    rw = lax.axis_index("rows")
    pix = rows * cols
    per_group = chans // GROUPS

    loads = [pltpu.make_async_copy(feat.at[f], fx.at[2 + f, 1:rows + 1], lsem.at[f]) for f in range(frames)]
    for c in loads:
        c.start()
    small = [pltpu.make_async_copy(p, par.at[i], psem.at[i]) for i, p in enumerate((g1, b1, c1, g2, b2, c2))]
    for c in small:
        c.start()
    taps = [
        pltpu.make_async_copy(w.at[:, e], v.at[:, :, e * chans:(e + 1) * chans], wsem.at[n, e])
        for n, (w, v) in enumerate(((w1, wa), (w2, wb))) for e in range(3)
    ]
    for c in taps:
        c.start()

    tb[...] = jnp.zeros_like(tb)

    barrier = pltpu.get_barrier_semaphore()
    for k in range(1, n_rw):
        pl.semaphore_signal(barrier, 1, device_id=(tm, lax.rem(rw + k, n_rw)), device_id_type=MESH)
    for k in range(1, n_tm):
        pl.semaphore_signal(barrier, 1, device_id=(lax.rem(tm + k, n_tm), rw), device_id_type=MESH)

    def frame_sums(z):
        part1 = jnp.sum(z.reshape(z.shape[0] // 8, 8, chans), axis=0)
        part2 = jnp.sum((z * z).reshape(z.shape[0] // 8, 8, chans), axis=0)
        return part1, part2

    def put_sums(which, f, part1, part2):
        sl[which, pl.ds(f, 1), :] = jnp.sum(part1, axis=0, keepdims=True)
        sl[which, pl.ds(frames + f, 1), :] = jnp.sum(part2, axis=0, keepdims=True)

    for f in range(frames):
        loads[f].wait()

        def add_row(r, carry, f=f):
            one, two = frame_sums(fx[2 + f, pl.ds(1 + 4 * r, 4)].reshape(4 * cols, chans).astype(jnp.float32))
            return carry[0] + one, carry[1] + two

        zero = jnp.zeros((8, chans), jnp.float32)
        one, two = lax.fori_loop(0, rows // 4, add_row, (zero, zero))
        put_sums(0, f, one, two)

    pl.semaphore_wait(barrier, n_rw - 1 + n_tm - 1)

    quarter = rows // 4

    def halo(buf, n, kind, e):
        def remote(src, dst, dev):
            return pltpu.make_async_remote_copy(
                src_ref=src, dst_ref=dst, send_sem=hsend.at[n, kind, e], recv_sem=hrecv.at[n, kind, e],
                device_id=dev, device_id_type=MESH)
        if kind == 0:
            return remote(buf.at[e, rows], buf.at[e, 0], (tm, rw + 1))
        if kind == 1:
            return remote(buf.at[e, 1], buf.at[e, rows + 1], (tm, rw - 1))
        part = pl.ds(1 + (kind - 2) * quarter, quarter)
        return remote(buf.at[e + frames, part], buf.at[e, part], (tm + 1, rw))

    ROW, TIME, EDGES, MIDDLE = (0, 1), (2, 3, 4, 5), (2, 5), (3, 4)
    sends = ((rw < n_rw - 1), (rw > 0)) + (tm < n_tm - 1,) * 4
    gets = ((rw > 0), (rw < n_rw - 1)) + (tm > 0,) * 4

    def halo_start(buf, n, kinds, e):
        for kind in kinds:
            @pl.when(sends[kind])
            def _():
                halo(buf, n, kind, e).start()

    def halo_sent(buf, n, kinds, e):
        for kind in kinds:
            @pl.when(sends[kind])
            def _():
                halo(buf, n, kind, e).wait_send()

    def halo_here(buf, n, kinds, e):
        for kind in kinds:
            @pl.when(gets[kind])
            def _():
                halo(buf, n, kind, e).wait_recv()

    def halo_edge(buf, n, e):
        @pl.when(tm > 0)
        def _():
            halo_start(buf, n, ROW, e)

    def halo_corner(buf, n, e):
        @pl.when(tm > 0)
        def _():
            halo_here(buf, n, ROW, e)

    place = lax.broadcasted_iota(jnp.int32, (2 * frames, chans), 0)
    keep = (lax.broadcasted_iota(jnp.int32, (2 * frames, chans), 1) % per_group) == place

    def pack(x):
        return jnp.sum(jnp.where(keep, group_sum(x, per_group), 0.0), axis=0, keepdims=True)

    def unpack(line):
        return group_sum(jnp.where(keep, line, 0.0), per_group)

    def row_copy(n, k):
        return pltpu.make_async_remote_copy(
            src_ref=ln.at[n], dst_ref=ra.at[n, k - 1], send_sem=rsend.at[n, k - 1], recv_sem=rrecv.at[n, k - 1],
            device_id=(tm, lax.rem(rw + k, n_rw)), device_id_type=MESH)

    def time_copy(n, k):
        return pltpu.make_async_remote_copy(
            src_ref=ln.at[2 + n], dst_ref=tb.at[n, k - 1], send_sem=tsend.at[n, k - 1], recv_sem=trecv.at[n, k - 1],
            device_id=(tm + k, rw), device_id_type=MESH)

    def stats_start(n):
        ln[n] = pack(sl[n])
        for k in (4, 5, 3, 2, 6, 7, 1):
            row_copy(n, k).start()

    def stats_finish(n, gain, shift, rest):
        for k in range(1, n_rw):
            row_copy(n, k).wait_recv()
        line = ln[n] + jnp.sum(ra[n], axis=0)
        ln[2 + n] = line
        for k in (10, 6, 9, 11, 14, 2, 5, 7, 8, 12, 13, 15, 3, 4, 1):
            @pl.when(tm + k < n_tm)
            def _():
                time_copy(n, k).start()
        rest()
        for k in range(1, n_tm):
            @pl.when(tm >= k)
            def _():
                time_copy(n, k).wait_recv()
        far, near, mine = unpack(jnp.sum(tb[n, 1:], axis=0)), unpack(tb[n, 0]), unpack(line)

        def running(lo):
            total = jnp.sum(far[lo:lo + frames], axis=0, keepdims=True)
            for f in range(frames - 1):
                total = total + near[lo + f:lo + f + 1]
            result = [total]
            total = total + near[lo + frames - 1:lo + frames]
            result.append(total)
            for f in range(frames):
                total = total + mine[lo + f:lo + f + 1]
                result.append(total)
            pad = jnp.zeros((8 - len(result), chans), jnp.float32)
            return jnp.concatenate(result + [pad], axis=0)

        one, two = running(0), running(frames)
        count = jnp.maximum(tm * frames + place - 1, 1).astype(jnp.float32) * float(n_rw * pix * per_group)
        mean = one / count
        var = two / count - mean * mean
        st[0] = mean
        st[1] = lax.rsqrt(var + EPSILON) * (0.5 * gain)
        st[2, 0:1] = 0.5 * shift

    def stats_sent(n):
        for k in range(1, n_rw):
            row_copy(n, k).wait_send()
        for k in range(1, n_tm):
            @pl.when(tm + k < n_tm)
            def _():
                time_copy(n, k).wait_send()

    def normalise(buf, e):
        mean, scale, shift = st[0, pl.ds(e, 1), :], st[1, pl.ds(e, 1), :], st[2, 0:1]

        def one(r):
            half = (buf[e, r].astype(jnp.float32) - mean) * scale + shift
            xn[e, pl.ds(pl.multiple_of(r * cols, cols), cols), :] = (half + half * jnp.tanh(half)).astype(jnp.bfloat16)

        def nothing(r):
            xn[e, pl.ds(r * cols, cols), :] = jnp.zeros((cols, chans), jnp.bfloat16)

        there = (tm > 0) | (e >= 2)

        @pl.when(there)
        def _():
            def four(i, _):
                for r in range(1, 5):
                    one(r + 4 * i)
                return 0
            lax.fori_loop(0, rows // 4, four, 0)

        @pl.when(there & (rw > 0))
        def _():
            one(0)

        @pl.when(there & (rw < n_rw - 1))
        def _():
            one(rows + 1)

        @pl.when(jnp.logical_not(there))
        def _():
            xn[e] = jnp.zeros_like(xn[e])

        @pl.when(there & (rw == 0))
        def _():
            nothing(0)

        @pl.when(there & (rw == n_rw - 1))
        def _():
            nothing(rows + 1)

    def time_taps(w, v):
        for a in range(3):
            outer = (w[a * 3].astype(jnp.float32) + w[a * 3 + 2].astype(jnp.float32)) * 0.5
            inner = w[a * 3 + 1].astype(jnp.float32) * 0.5
            v[a] = (outer - inner).astype(jnp.bfloat16)
            w[a * 3 + 1] = (outer + inner).astype(jnp.bfloat16)

    def frame(e):
        return xn[e].astype(jnp.float32)

    col = lax.broadcasted_iota(jnp.int32, (pix, chans), 0) % cols

    def product(w, v, k, e):
        total = None
        for a in range(3):
            tap = (w.at[a * 3], w.at[a * 3 + 1], v.at[a], w.at[a * 3 + 2])[k]
            part = jnp.dot(un[k, a * cols:a * cols + pix, :], tap[:, e * chans:(e + 1) * chans],
                           preferred_element_type=jnp.float32)
            total = part if total is None else total + part
        return total

    def column(y, e):
        if e == 0:
            return jnp.where(col == 0, 0.0, pltpu.roll(y, 1, 0))
        if e == 2:
            return jnp.where(col == cols - 1, 0.0, pltpu.roll(y, pix - 1, 0))
        return y

    def conv_late(w, v, f, bias):
        d1, d2, d3 = frame(f + 1), frame(f + 2), frame(f + 3)
        un[1] = (d1 + d2).astype(jnp.bfloat16)
        un[2] = (d2 - d1).astype(jnp.bfloat16)
        un[3] = (d1 - d3).astype(jnp.bfloat16)
        y0 = y1 = bias
        for e in (1, 0, 2):
            m1, m2, m3 = [product(w, v, k, e) for k in (1, 2, 3)]
            y0, y1 = y0 + column(m1 + m2, e), y1 + column(m1 - m2 - m3, e)
        acc[...] = y0
        return y1

    def conv_early(w, v, f):
        un[0] = (frame(f) - frame(f + 2)).astype(jnp.bfloat16)
        y = acc[...]
        for e in (1, 0, 2):
            y = y + column(product(w, v, 0, e), e)
        return y

    stats_start(0)
    for e in range(2, 2 + frames):
        halo_start(fx, 0, ROW, e)
    halo_start(fx, 0, EDGES[:1], 1)
    for c in small:
        c.wait()
    for c in taps[:3]:
        c.wait()
    time_taps(wa, va)

    def rest_first():
        halo_start(fx, 0, EDGES[1:], 1)
        halo_start(fx, 0, EDGES, 0)
        halo_start(fx, 0, MIDDLE[:1], 1)
        for c in taps[3:]:
            c.wait()
        time_taps(wb, vb)

    def edges_on(buf, n):
        for e in (1, 0):
            halo_here(buf, n, EDGES, e)
            halo_edge(buf, n, e)

    stats_finish(0, par[0], par[1], rest_first)
    for e in range(2, 2 + frames):
        halo_here(fx, 0, ROW, e)
        normalise(fx, e)
    edges_on(fx, 0)
    halo_start(fx, 0, MIDDLE[1:], 1)
    halo_start(fx, 0, MIDDLE, 0)

    def earlier(buf, n, i, e):
        @pl.when(i == 1)
        def _():
            halo_here(buf, n, MIDDLE, e)
            halo_corner(buf, n, e)
            normalise(buf, e)

    def first_conv(i, _):
        f = 2 - 2 * i

        def put(g, y):
            y = y.astype(jnp.bfloat16)
            bx[2 + g, 1:rows + 1] = y.reshape(rows, cols, chans)
            put_sums(1, g, *frame_sums(y.astype(jnp.float32)))
            halo_start(bx, 1, ROW, 2 + g)

        earlier(fx, 0, i, 1)
        put(f + 1, conv_late(wa, va, f, par[2]))

        @pl.when(i == 0)
        def _():
            halo_start(bx, 1, EDGES, 1)

        earlier(fx, 0, i, 0)
        put(f, conv_early(wa, va, f))
        return 0

    lax.fori_loop(0, 2, first_conv, 0)

    def rest_second():
        halo_start(bx, 1, EDGES[1:], 0)
        halo_start(bx, 1, MIDDLE[:1], 1)

    stats_start(1)
    halo_start(bx, 1, EDGES[:1], 0)
    stats_finish(1, par[3], par[4], rest_second)
    edges_on(bx, 1)
    halo_start(bx, 1, MIDDLE[1:], 1)
    halo_start(bx, 1, MIDDLE, 0)
    for e in range(2, 2 + frames):
        halo_here(bx, 1, ROW, e)
        normalise(bx, e)

    def second_conv(i, _):
        f = 2 - 2 * i

        def put(g, y):
            y = y + fx[2 + g, 1:rows + 1].reshape(pix, chans).astype(jnp.float32)
            out[g] = y.astype(jnp.bfloat16).reshape(rows, cols, chans)

        earlier(bx, 1, i, 1)
        put(f + 1, conv_late(wb, vb, f, par[5]))
        earlier(bx, 1, i, 0)
        put(f, conv_early(wb, vb, f))
        return 0

    lax.fori_loop(0, 2, second_conv, 0)

    for n, buf in enumerate((fx, bx)):
        for e in (1, 0):
            halo_sent(buf, n, TIME, e)

            @pl.when(tm > 0)
            def _():
                halo_sent(buf, n, ROW, e)
        for e in range(2, 2 + frames):
            halo_sent(buf, n, ROW, e)
        stats_sent(n)


def solution(mesh):
    n_tm, n_rw = mesh.shape["tm"], mesh.shape["rows"]

    def on_device(features, gamma_one, beta_one, weight_one, bias_one, gamma_two, beta_two, weight_two, bias_two):
        frames, rows, cols, chans = features.shape
        taps = lambda w: w.reshape(9, 3, chans, chans)
        line = lambda v: v.reshape(1, chans)
        bf16, f32 = jnp.bfloat16, jnp.float32
        dma = pltpu.SemaphoreType.DMA
        return pl.pallas_call(
            functools.partial(block_kernel, n_tm, n_rw, frames, rows, cols, chans),
            out_shape=jax.ShapeDtypeStruct(features.shape, bf16),
            in_specs=[HBM] * 9,
            out_specs=pl.BlockSpec(memory_space=pltpu.VMEM),
            scratch_shapes=[
                pltpu.VMEM((frames + 2, rows + 2, cols, chans), bf16),
                pltpu.VMEM((frames + 2, rows + 2, cols, chans), bf16),
                pltpu.VMEM((frames + 2, (rows + 2) * cols, chans), bf16),
                pltpu.VMEM((4, (rows + 2) * cols, chans), bf16),
                pltpu.VMEM((rows * cols, chans), f32),
                pltpu.VMEM((9, chans, 3 * chans), bf16),
                pltpu.VMEM((9, chans, 3 * chans), bf16),
                pltpu.VMEM((3, chans, 3 * chans), bf16),
                pltpu.VMEM((3, chans, 3 * chans), bf16),
                pltpu.VMEM((6, 1, chans), f32),
                pltpu.VMEM((2, 2 * frames, chans), f32),
                pltpu.VMEM((4, 1, chans), f32),
                pltpu.VMEM((2, n_rw - 1, 1, chans), f32),
                pltpu.VMEM((2, n_tm - 1, 1, chans), f32),
                pltpu.VMEM((3, 8, chans), f32),
                dma((frames,)), dma((6,)), dma((2, 3)),
                dma((2, n_rw - 1)), dma((2, n_rw - 1)), dma((2, n_tm - 1)), dma((2, n_tm - 1)),
                dma((2, 6, frames + 2)), dma((2, 6, frames + 2)),
            ],
            compiler_params=pltpu.CompilerParams(
                collective_id=0, has_side_effects=True, vmem_limit_bytes=52 << 20),
        )(*[pltpu.with_memory_space_constraint(v, pltpu.HBM) for v in (
            features, line(gamma_one), line(beta_one), taps(weight_one), line(bias_one),
            line(gamma_two), line(beta_two), taps(weight_two), line(bias_two))])

    placed = (P("tm", "rows", None, None), P(), P(), P(), P(), P(), P(), P(), P())
    return jax.shard_map(on_device, mesh=mesh, in_specs=placed, out_specs=P("tm", "rows", None, None), check_vma=False)
```

```python
import functools

import jax
import jax.numpy as jnp
from jax import lax
from jax.experimental import pallas as pl
from jax.experimental.pallas import tpu as pltpu
from jax.sharding import PartitionSpec as P

MESH = pl.DeviceIdType.MESH
GROUPS = 32
EPSILON = 1e-06
RING = 4
HBM = pl.BlockSpec(memory_space=pltpu.HBM)


def group_sum(x, per_group):
    lane = lax.broadcasted_iota(jnp.int32, x.shape, 1)
    step = 1
    while step < per_group:
        up = pltpu.roll(x, x.shape[1] - step, 1)
        down = pltpu.roll(x, step, 1)
        x = x + jnp.where((lane & step) == 0, up, down)
        step *= 2
    return x


def block_kernel(n_tm, n_rw, frames, rows, cols, chans,
                 feat, g1, b1, w1, c1, g2, b2, w2, c2, out,
                 fx, bx, xn, un, acc, wa, wb, va, vb, par, sl, ln, ra, tb, st, rel,
                 lsem, psem, wsem, rsend, rrecv, tsend, trecv, hsend, hrecv, gsend, grecv):
    tm = lax.axis_index("tm")
    rw = lax.axis_index("rows")
    pix = rows * cols
    per_group = chans // GROUPS

    loads = [pltpu.make_async_copy(feat.at[f], fx.at[2 + f, 1:rows + 1], lsem.at[f]) for f in range(frames)]
    for c in loads:
        c.start()
    small = [pltpu.make_async_copy(p, par.at[i], psem.at[i]) for i, p in enumerate((g1, b1, c1, g2, b2, c2))]
    for c in small:
        c.start()
    taps = [
        pltpu.make_async_copy(w.at[:, e], v.at[:, :, e * chans:(e + 1) * chans], wsem.at[n, e])
        for n, (w, v) in enumerate(((w1, wa), (w2, wb))) for e in range(3)
    ]
    for c in taps:
        c.start()

    tb[...] = jnp.zeros_like(tb)

    barrier = pltpu.get_barrier_semaphore()
    for k in range(1, n_rw):
        pl.semaphore_signal(barrier, 1, device_id=(tm, lax.rem(rw + k, n_rw)), device_id_type=MESH)
    for k in range(1, n_tm):
        pl.semaphore_signal(barrier, 1, device_id=(lax.rem(tm + k, n_tm), rw), device_id_type=MESH)

    def frame_sums(z):
        part1 = jnp.sum(z.reshape(z.shape[0] // 8, 8, chans), axis=0)
        part2 = jnp.sum((z * z).reshape(z.shape[0] // 8, 8, chans), axis=0)
        return part1, part2

    def put_sums(which, f, part1, part2):
        sl[which, pl.ds(f, 1), :] = jnp.sum(part1, axis=0, keepdims=True)
        sl[which, pl.ds(frames + f, 1), :] = jnp.sum(part2, axis=0, keepdims=True)

    for f in range(frames):
        loads[f].wait()

        def add_row(r, carry, f=f):
            one, two = frame_sums(fx[2 + f, pl.ds(1 + 4 * r, 4)].reshape(4 * cols, chans).astype(jnp.float32))
            return carry[0] + one, carry[1] + two

        zero = jnp.zeros((8, chans), jnp.float32)
        one, two = lax.fori_loop(0, rows // 4, add_row, (zero, zero))
        put_sums(0, f, one, two)

    pl.semaphore_wait(barrier, n_rw - 1 + n_tm - 1)

    quarter = rows // 4

    def halo(buf, n, kind, e):
        def remote(src, dst, dev):
            return pltpu.make_async_remote_copy(
                src_ref=src, dst_ref=dst, send_sem=hsend.at[n, kind, e], recv_sem=hrecv.at[n, kind, e],
                device_id=dev, device_id_type=MESH)
        if kind == 0:
            return remote(buf.at[e, rows], buf.at[e, 0], (tm, rw + 1))
        if kind == 1:
            return remote(buf.at[e, 1], buf.at[e, rows + 1], (tm, rw - 1))
        part = pl.ds(1 + (kind - 2) * quarter, quarter)
        return remote(buf.at[e + frames, part], buf.at[e, part], (tm + 1, rw))

    ROW, TIME, EDGES, MIDDLE = (0, 1), (2, 3, 4, 5), (2, 5), (3, 4)
    sends = ((rw < n_rw - 1), (rw > 0)) + (tm < n_tm - 1,) * 4
    gets = ((rw > 0), (rw < n_rw - 1)) + (tm > 0,) * 4

    def halo_start(buf, n, kinds, e):
        for kind in kinds:
            @pl.when(sends[kind])
            def _():
                halo(buf, n, kind, e).start()

    def halo_sent(buf, n, kinds, e):
        for kind in kinds:
            @pl.when(sends[kind])
            def _():
                halo(buf, n, kind, e).wait_send()

    def halo_here(buf, n, kinds, e):
        for kind in kinds:
            @pl.when(gets[kind])
            def _():
                halo(buf, n, kind, e).wait_recv()

    LONG = ((4, 0), (4, 1))

    def ring(step):
        return tm - lax.rem(tm, RING) + lax.rem(tm + step, RING)

    def long_copy(buf, n, hop):
        kind, e = LONG[n]
        part = pl.ds(1 + (kind - 2) * quarter, quarter)
        src = (buf.at[e + frames, part], rel.at[n, 0], rel.at[n, 1])[hop]
        dst = (rel.at[n, 0], rel.at[n, 1], buf.at[e, part])[hop]
        return pltpu.make_async_remote_copy(
            src_ref=src, dst_ref=dst, send_sem=gsend.at[n, hop],
            recv_sem=hrecv.at[n, kind, e] if hop == 2 else grecv.at[n, hop],
            device_id=(ring(2) + 1 if hop == 2 else ring(RING - 1), rw), device_id_type=MESH)

    def long_start(buf, n, hop):
        @pl.when(ring(hop) < n_tm - 1)
        def _():
            if hop:
                long_copy(buf, n, hop - 1).wait_recv()
            long_copy(buf, n, hop).start()

    def long_sent(buf, n):
        for hop in range(3):
            @pl.when(ring(hop) < n_tm - 1)
            def _():
                long_copy(buf, n, hop).wait_send()

    def halo_edge(buf, n, e):
        @pl.when(tm > 0)
        def _():
            halo_start(buf, n, ROW, e)

    def halo_corner(buf, n, e):
        @pl.when(tm > 0)
        def _():
            halo_here(buf, n, ROW, e)

    place = lax.broadcasted_iota(jnp.int32, (2 * frames, chans), 0)
    keep = (lax.broadcasted_iota(jnp.int32, (2 * frames, chans), 1) % per_group) == place

    def pack(x):
        return jnp.sum(jnp.where(keep, group_sum(x, per_group), 0.0), axis=0, keepdims=True)

    def unpack(line):
        return group_sum(jnp.where(keep, line, 0.0), per_group)

    def row_copy(n, k):
        return pltpu.make_async_remote_copy(
            src_ref=ln.at[n], dst_ref=ra.at[n, k - 1], send_sem=rsend.at[n, k - 1], recv_sem=rrecv.at[n, k - 1],
            device_id=(tm, lax.rem(rw + k, n_rw)), device_id_type=MESH)

    def time_copy(n, k):
        return pltpu.make_async_remote_copy(
            src_ref=ln.at[2 + n], dst_ref=tb.at[n, k - 1], send_sem=tsend.at[n, k - 1], recv_sem=trecv.at[n, k - 1],
            device_id=(tm + k, rw), device_id_type=MESH)

    def stats_start(n):
        ln[n] = pack(sl[n])
        for k in (4, 5, 3, 2, 6, 7, 1):
            row_copy(n, k).start()

    def stats_finish(n, gain, shift, rest):
        for k in range(1, n_rw):
            row_copy(n, k).wait_recv()
        line = ln[n] + jnp.sum(ra[n], axis=0)
        ln[2 + n] = line
        for k in (10, 6, 9, 11, 14, 2, 5, 7, 8, 12, 13, 15, 3, 4, 1):
            @pl.when(tm + k < n_tm)
            def _():
                time_copy(n, k).start()
        rest()
        for k in range(1, n_tm):
            @pl.when(tm >= k)
            def _():
                time_copy(n, k).wait_recv()
        far, near, mine = unpack(jnp.sum(tb[n, 1:], axis=0)), unpack(tb[n, 0]), unpack(line)

        def running(lo):
            total = jnp.sum(far[lo:lo + frames], axis=0, keepdims=True)
            for f in range(frames - 1):
                total = total + near[lo + f:lo + f + 1]
            result = [total]
            total = total + near[lo + frames - 1:lo + frames]
            result.append(total)
            for f in range(frames):
                total = total + mine[lo + f:lo + f + 1]
                result.append(total)
            pad = jnp.zeros((8 - len(result), chans), jnp.float32)
            return jnp.concatenate(result + [pad], axis=0)

        one, two = running(0), running(frames)
        count = jnp.maximum(tm * frames + place - 1, 1).astype(jnp.float32) * float(n_rw * pix * per_group)
        mean = one / count
        var = two / count - mean * mean
        st[0] = mean
        st[1] = lax.rsqrt(var + EPSILON) * (0.5 * gain)
        st[2, 0:1] = 0.5 * shift

    def stats_sent(n):
        for k in range(1, n_rw):
            row_copy(n, k).wait_send()
        for k in range(1, n_tm):
            @pl.when(tm + k < n_tm)
            def _():
                time_copy(n, k).wait_send()

    def normalise(buf, e):
        mean, scale, shift = st[0, pl.ds(e, 1), :], st[1, pl.ds(e, 1), :], st[2, 0:1]

        def one(r):
            half = (buf[e, r].astype(jnp.float32) - mean) * scale + shift
            xn[e, pl.ds(pl.multiple_of(r * cols, cols), cols), :] = (half + half * jnp.tanh(half)).astype(jnp.bfloat16)

        def nothing(r):
            xn[e, pl.ds(r * cols, cols), :] = jnp.zeros((cols, chans), jnp.bfloat16)

        there = (tm > 0) | (e >= 2)

        @pl.when(there)
        def _():
            def four(i, _):
                for r in range(1, 5):
                    one(r + 4 * i)
                return 0
            lax.fori_loop(0, rows // 4, four, 0)

        @pl.when(there & (rw > 0))
        def _():
            one(0)

        @pl.when(there & (rw < n_rw - 1))
        def _():
            one(rows + 1)

        @pl.when(jnp.logical_not(there))
        def _():
            xn[e] = jnp.zeros_like(xn[e])

        @pl.when(there & (rw == 0))
        def _():
            nothing(0)

        @pl.when(there & (rw == n_rw - 1))
        def _():
            nothing(rows + 1)

    def time_taps(w, v):
        for a in range(3):
            outer = (w[a * 3].astype(jnp.float32) + w[a * 3 + 2].astype(jnp.float32)) * 0.5
            inner = w[a * 3 + 1].astype(jnp.float32) * 0.5
            v[a] = (outer - inner).astype(jnp.bfloat16)
            w[a * 3 + 1] = (outer + inner).astype(jnp.bfloat16)

    def frame(e):
        return xn[e].astype(jnp.float32)

    col = lax.broadcasted_iota(jnp.int32, (pix, chans), 0) % cols

    def product(w, v, k, e):
        total = None
        for a in range(3):
            tap = (w.at[a * 3], w.at[a * 3 + 1], v.at[a], w.at[a * 3 + 2])[k]
            part = jnp.dot(un[k, a * cols:a * cols + pix, :], tap[:, e * chans:(e + 1) * chans],
                           preferred_element_type=jnp.float32)
            total = part if total is None else total + part
        return total

    def column(y, e):
        if e == 0:
            return jnp.where(col == 0, 0.0, pltpu.roll(y, 1, 0))
        if e == 2:
            return jnp.where(col == cols - 1, 0.0, pltpu.roll(y, pix - 1, 0))
        return y

    def conv_late(w, v, f, bias):
        d1, d2, d3 = frame(f + 1), frame(f + 2), frame(f + 3)
        un[1] = (d1 + d2).astype(jnp.bfloat16)
        un[2] = (d2 - d1).astype(jnp.bfloat16)
        un[3] = (d1 - d3).astype(jnp.bfloat16)
        y0 = y1 = bias
        for e in (1, 0, 2):
            m1, m2, m3 = [product(w, v, k, e) for k in (1, 2, 3)]
            y0, y1 = y0 + column(m1 + m2, e), y1 + column(m1 - m2 - m3, e)
        acc[...] = y0
        return y1

    def conv_early(w, v, f):
        un[0] = (frame(f) - frame(f + 2)).astype(jnp.bfloat16)
        y = acc[...]
        for e in (1, 0, 2):
            y = y + column(product(w, v, 0, e), e)
        return y

    stats_start(0)
    for e in range(2, 2 + frames):
        halo_start(fx, 0, ROW, e)
    halo_start(fx, 0, EDGES, 1)
    halo_start(fx, 0, EDGES[:1], 0)
    long_start(fx, 0, 0)
    for c in small:
        c.wait()
    for c in taps[:3]:
        c.wait()
    time_taps(wa, va)

    def rest_first():
        halo_start(fx, 0, EDGES[1:], 0)
        halo_start(fx, 0, MIDDLE, 1)
        for c in taps[3:]:
            c.wait()
        time_taps(wb, vb)
        long_start(fx, 0, 1)

    def edges_on(buf, n):
        for e in (1, 0):
            halo_here(buf, n, EDGES, e)
            halo_edge(buf, n, e)

    stats_finish(0, par[0], par[1], rest_first)
    for e in range(2, 2 + frames):
        halo_here(fx, 0, ROW, e)
        normalise(fx, e)
    edges_on(fx, 0)
    halo_start(fx, 0, MIDDLE[:1], 0)
    long_start(fx, 0, 2)

    def earlier(buf, n, i, e):
        @pl.when(i == 1)
        def _():
            halo_here(buf, n, MIDDLE, e)
            halo_corner(buf, n, e)
            normalise(buf, e)

    def first_conv(i, _):
        f = 2 - 2 * i

        def put(g, y):
            y = y.astype(jnp.bfloat16)
            bx[2 + g, 1:rows + 1] = y.reshape(rows, cols, chans)
            put_sums(1, g, *frame_sums(y.astype(jnp.float32)))
            halo_start(bx, 1, ROW, 2 + g)

        earlier(fx, 0, i, 1)
        put(f + 1, conv_late(wa, va, f, par[2]))

        @pl.when(i == 0)
        def _():
            halo_start(bx, 1, EDGES, 1)
            long_start(bx, 1, 0)

        @pl.when(i == 1)
        def _():
            long_start(bx, 1, 1)

        earlier(fx, 0, i, 0)
        put(f, conv_early(wa, va, f))
        return 0

    lax.fori_loop(0, 2, first_conv, 0)

    def rest_second():
        halo_start(bx, 1, EDGES[1:], 0)
        halo_start(bx, 1, MIDDLE[:1], 1)
        long_start(bx, 1, 2)

    stats_start(1)
    halo_start(bx, 1, EDGES[:1], 0)
    stats_finish(1, par[3], par[4], rest_second)
    edges_on(bx, 1)
    halo_start(bx, 1, MIDDLE, 0)
    for e in range(2, 2 + frames):
        halo_here(bx, 1, ROW, e)
        normalise(bx, e)

    def second_conv(i, _):
        f = 2 - 2 * i

        def put(g, y):
            y = y + fx[2 + g, 1:rows + 1].reshape(pix, chans).astype(jnp.float32)
            out[g] = y.astype(jnp.bfloat16).reshape(rows, cols, chans)

        earlier(bx, 1, i, 1)
        put(f + 1, conv_late(wb, vb, f, par[5]))
        earlier(bx, 1, i, 0)
        put(f, conv_early(wb, vb, f))
        return 0

    lax.fori_loop(0, 2, second_conv, 0)

    for n, buf in enumerate((fx, bx)):
        for e in (1, 0):
            halo_sent(buf, n, [kind for kind in TIME if (kind, e) != LONG[n]], e)

            @pl.when(tm > 0)
            def _():
                halo_sent(buf, n, ROW, e)
        for e in range(2, 2 + frames):
            halo_sent(buf, n, ROW, e)
        stats_sent(n)
        long_sent(buf, n)


def solution(mesh):
    n_tm, n_rw = mesh.shape["tm"], mesh.shape["rows"]

    def on_device(features, gamma_one, beta_one, weight_one, bias_one, gamma_two, beta_two, weight_two, bias_two):
        frames, rows, cols, chans = features.shape
        taps = lambda w: w.reshape(9, 3, chans, chans)
        line = lambda v: v.reshape(1, chans)
        bf16, f32 = jnp.bfloat16, jnp.float32
        dma = pltpu.SemaphoreType.DMA
        return pl.pallas_call(
            functools.partial(block_kernel, n_tm, n_rw, frames, rows, cols, chans),
            out_shape=jax.ShapeDtypeStruct(features.shape, bf16),
            in_specs=[HBM] * 9,
            out_specs=pl.BlockSpec(memory_space=pltpu.VMEM),
            scratch_shapes=[
                pltpu.VMEM((frames + 2, rows + 2, cols, chans), bf16),
                pltpu.VMEM((frames + 2, rows + 2, cols, chans), bf16),
                pltpu.VMEM((frames + 2, (rows + 2) * cols, chans), bf16),
                pltpu.VMEM((4, (rows + 2) * cols, chans), bf16),
                pltpu.VMEM((rows * cols, chans), f32),
                pltpu.VMEM((9, chans, 3 * chans), bf16),
                pltpu.VMEM((9, chans, 3 * chans), bf16),
                pltpu.VMEM((3, chans, 3 * chans), bf16),
                pltpu.VMEM((3, chans, 3 * chans), bf16),
                pltpu.VMEM((6, 1, chans), f32),
                pltpu.VMEM((2, 2 * frames, chans), f32),
                pltpu.VMEM((4, 1, chans), f32),
                pltpu.VMEM((2, n_rw - 1, 1, chans), f32),
                pltpu.VMEM((2, n_tm - 1, 1, chans), f32),
                pltpu.VMEM((3, 8, chans), f32),
                pltpu.VMEM((2, 2, rows // 4, cols, chans), bf16),
                dma((frames,)), dma((6,)), dma((2, 3)),
                dma((2, n_rw - 1)), dma((2, n_rw - 1)), dma((2, n_tm - 1)), dma((2, n_tm - 1)),
                dma((2, 6, frames + 2)), dma((2, 6, frames + 2)), dma((2, 3)), dma((2, 2)),
            ],
            compiler_params=pltpu.CompilerParams(
                collective_id=0, has_side_effects=True, vmem_limit_bytes=52 << 20),
        )(*[pltpu.with_memory_space_constraint(v, pltpu.HBM) for v in (
            features, line(gamma_one), line(beta_one), taps(weight_one), line(bias_one),
            line(gamma_two), line(beta_two), taps(weight_two), line(bias_two))])

    placed = (P("tm", "rows", None, None), P(), P(), P(), P(), P(), P(), P(), P())
    return jax.shard_map(on_device, mesh=mesh, in_specs=placed, out_specs=P("tm", "rows", None, None), check_vma=False)
```

```python
import functools

import jax
import jax.numpy as jnp
from jax import lax
from jax.experimental import pallas as pl
from jax.experimental.pallas import tpu as pltpu
from jax.sharding import PartitionSpec as P

MESH = pl.DeviceIdType.MESH
GROUPS = 32
EPSILON = 1e-06
RING = 4
HBM = pl.BlockSpec(memory_space=pltpu.HBM)


def group_sum(x, per_group):
    lane = lax.broadcasted_iota(jnp.int32, x.shape, 1)
    step = 1
    while step < per_group:
        up = pltpu.roll(x, x.shape[1] - step, 1)
        down = pltpu.roll(x, step, 1)
        x = x + jnp.where((lane & step) == 0, up, down)
        step *= 2
    return x


def block_kernel(n_tm, n_rw, frames, rows, cols, chans,
                 feat, g1, b1, w1, c1, g2, b2, w2, c2, out,
                 fx, bx, xn, un, acc, wa, wb, va, vb, par, sl, ln, lt, ra, tb, st, rel,
                 lsem, psem, wsem, rsend, rrecv, tsend, trecv, hsend, hrecv, gsend, grecv):
    tm = lax.axis_index("tm")
    rw = lax.axis_index("rows")
    pix = rows * cols
    per_group = chans // GROUPS

    loads = [pltpu.make_async_copy(feat.at[f], fx.at[2 + f, 1:rows + 1], lsem.at[f]) for f in range(frames)]
    for c in loads:
        c.start()
    small = [pltpu.make_async_copy(p, par.at[i], psem.at[i]) for i, p in enumerate((g1, b1, c1, g2, b2, c2))]
    for c in small:
        c.start()
    taps = [
        pltpu.make_async_copy(w.at[:, e], v.at[:, :, e * chans:(e + 1) * chans], wsem.at[n, e])
        for n, (w, v) in enumerate(((w1, wa), (w2, wb))) for e in range(3)
    ]
    for c in taps:
        c.start()

    barrier = pltpu.get_barrier_semaphore()
    for k in range(1, n_rw):
        pl.semaphore_signal(barrier, 1, device_id=(tm, lax.rem(rw + k, n_rw)), device_id_type=MESH)
    for k in range(1, n_tm):
        pl.semaphore_signal(barrier, 1, device_id=(lax.rem(tm + k, n_tm), rw), device_id_type=MESH)

    def frame_sums(z):
        part1 = jnp.sum(z.reshape(z.shape[0] // 8, 8, chans), axis=0)
        part2 = jnp.sum((z * z).reshape(z.shape[0] // 8, 8, chans), axis=0)
        return part1, part2

    def put_sums(which, f, part1, part2):
        sl[which, pl.ds(f, 1), :] = jnp.sum(part1, axis=0, keepdims=True)
        sl[which, pl.ds(frames + f, 1), :] = jnp.sum(part2, axis=0, keepdims=True)

    for f in range(frames):
        loads[f].wait()

        def add_row(r, carry, f=f):
            one, two = frame_sums(fx[2 + f, pl.ds(1 + 4 * r, 4)].reshape(4 * cols, chans).astype(jnp.float32))
            return carry[0] + one, carry[1] + two

        zero = jnp.zeros((8, chans), jnp.float32)
        one, two = lax.fori_loop(0, rows // 4, add_row, (zero, zero))
        put_sums(0, f, one, two)

    pl.semaphore_wait(barrier, n_rw - 1 + n_tm - 1)

    quarter = rows // 4

    def halo(buf, n, kind, e):
        def remote(src, dst, dev):
            return pltpu.make_async_remote_copy(
                src_ref=src, dst_ref=dst, send_sem=hsend.at[n, kind, e], recv_sem=hrecv.at[n, kind, e],
                device_id=dev, device_id_type=MESH)
        if kind == 0:
            return remote(buf.at[e, rows], buf.at[e, 0], (tm, rw + 1))
        if kind == 1:
            return remote(buf.at[e, 1], buf.at[e, rows + 1], (tm, rw - 1))
        part = pl.ds(1 + (kind - 2) * quarter, quarter)
        return remote(buf.at[e + frames, part], buf.at[e, part], (tm + 1, rw))

    ROW, TIME, EDGES, MIDDLE = (0, 1), (2, 3, 4, 5), (2, 5), (3, 4)
    sends = ((rw < n_rw - 1), (rw > 0)) + (tm < n_tm - 1,) * 4
    gets = ((rw > 0), (rw < n_rw - 1)) + (tm > 0,) * 4

    def halo_start(buf, n, kinds, e):
        for kind in kinds:
            @pl.when(sends[kind])
            def _():
                halo(buf, n, kind, e).start()

    def halo_sent(buf, n, kinds, e):
        for kind in kinds:
            @pl.when(sends[kind])
            def _():
                halo(buf, n, kind, e).wait_send()

    def halo_here(buf, n, kinds, e):
        for kind in kinds:
            @pl.when(gets[kind])
            def _():
                halo(buf, n, kind, e).wait_recv()

    LONG = ((4, 0), (4, 1))

    def ring(step):
        return tm - lax.rem(tm, RING) + lax.rem(tm + step, RING)

    def long_copy(buf, n, hop):
        kind, e = LONG[n]
        part = pl.ds(1 + (kind - 2) * quarter, quarter)
        src = (buf.at[e + frames, part], rel.at[n, 0], rel.at[n, 1])[hop]
        dst = (rel.at[n, 0], rel.at[n, 1], buf.at[e, part])[hop]
        return pltpu.make_async_remote_copy(
            src_ref=src, dst_ref=dst, send_sem=gsend.at[n, hop],
            recv_sem=hrecv.at[n, kind, e] if hop == 2 else grecv.at[n, hop],
            device_id=(ring(2) + 1 if hop == 2 else ring(RING - 1), rw), device_id_type=MESH)

    def long_start(buf, n, hop):
        @pl.when(ring(hop) < n_tm - 1)
        def _():
            if hop:
                long_copy(buf, n, hop - 1).wait_recv()
            long_copy(buf, n, hop).start()

    def long_sent(buf, n):
        for hop in range(3):
            @pl.when(ring(hop) < n_tm - 1)
            def _():
                long_copy(buf, n, hop).wait_send()

    def halo_edge(buf, n, e):
        @pl.when(tm > 0)
        def _():
            halo_start(buf, n, ROW, e)

    def halo_corner(buf, n, e):
        @pl.when(tm > 0)
        def _():
            halo_here(buf, n, ROW, e)

    place = lax.broadcasted_iota(jnp.int32, (2 * frames, chans), 0)
    keep = (lax.broadcasted_iota(jnp.int32, (2 * frames, chans), 1) % per_group) == place

    def pack(x):
        return jnp.sum(jnp.where(keep, group_sum(x, per_group), 0.0), axis=0, keepdims=True)

    def unpack(line):
        return group_sum(jnp.where(keep, line, 0.0), per_group)

    def row_copy(n, k):
        return pltpu.make_async_remote_copy(
            src_ref=lt.at[n], dst_ref=ra.at[n, k - 1], send_sem=rsend.at[n], recv_sem=rrecv.at[n],
            device_id=(tm, lax.rem(rw + k, n_rw)), device_id_type=MESH)

    def time_copy(n, k):
        return pltpu.make_async_remote_copy(
            src_ref=ln.at[n], dst_ref=tb.at[n, k - 1], send_sem=tsend.at[n], recv_sem=trecv.at[n],
            device_id=(lax.rem(tm + k, n_tm), rw), device_id_type=MESH)

    def all_rows(n):
        return pltpu.make_async_remote_copy(
            src_ref=ra.at[n], dst_ref=ra.at[n], send_sem=rsend.at[n], recv_sem=rrecv.at[n],
            device_id=(tm, lax.rem(rw + 1, n_rw)), device_id_type=MESH)

    def all_times(n):
        return pltpu.make_async_remote_copy(
            src_ref=tb.at[n], dst_ref=tb.at[n], send_sem=tsend.at[n], recv_sem=trecv.at[n],
            device_id=(lax.rem(tm + 1, n_tm), rw), device_id_type=MESH)

    def stats_start(n):
        ln[n] = pack(sl[n])
        for k in (10, 6, 9, 11, 14, 2, 5, 7, 8, 12, 13, 15, 3, 4, 1):
            time_copy(n, k).start()

    def stats_finish(n, gain, shift, meanwhile):
        all_times(n).wait_recv()
        ago = lax.broadcasted_iota(jnp.int32, (n_tm - 1, 1, chans), 0) + 1
        times = jnp.where(ago <= tm, tb[n], 0.0)
        lt[n, 0] = jnp.sum(times[1:], axis=0)
        lt[n, 1] = times[0]
        lt[n, 2] = ln[n]
        for k in (4, 5, 3, 2, 6, 7, 1):
            row_copy(n, k).start()
        meanwhile()
        all_rows(n).wait_recv()
        lines = lt[n] + jnp.sum(ra[n], axis=0)
        far, near, mine = unpack(lines[0]), unpack(lines[1]), unpack(lines[2])

        def running(lo):
            total = jnp.sum(far[lo:lo + frames], axis=0, keepdims=True)
            for f in range(frames - 1):
                total = total + near[lo + f:lo + f + 1]
            result = [total]
            total = total + near[lo + frames - 1:lo + frames]
            result.append(total)
            for f in range(frames):
                total = total + mine[lo + f:lo + f + 1]
                result.append(total)
            pad = jnp.zeros((8 - len(result), chans), jnp.float32)
            return jnp.concatenate(result + [pad], axis=0)

        one, two = running(0), running(frames)
        count = jnp.maximum(tm * frames + place - 1, 1).astype(jnp.float32) * float(n_rw * pix * per_group)
        mean = one / count
        var = two / count - mean * mean
        st[0] = mean
        st[1] = lax.rsqrt(var + EPSILON) * (0.5 * gain)
        st[2, 0:1] = 0.5 * shift

    def stats_sent(n):
        all_rows(n).wait_send()
        all_times(n).wait_send()

    def normalise(buf, e):
        mean, scale, shift = st[0, pl.ds(e, 1), :], st[1, pl.ds(e, 1), :], st[2, 0:1]

        def one(r):
            half = (buf[e, r].astype(jnp.float32) - mean) * scale + shift
            xn[e, pl.ds(pl.multiple_of(r * cols, cols), cols), :] = (half + half * jnp.tanh(half)).astype(jnp.bfloat16)

        def nothing(r):
            xn[e, pl.ds(r * cols, cols), :] = jnp.zeros((cols, chans), jnp.bfloat16)

        there = (tm > 0) | (e >= 2)

        @pl.when(there)
        def _():
            def four(i, _):
                for r in range(1, 5):
                    one(r + 4 * i)
                return 0
            lax.fori_loop(0, rows // 4, four, 0)

        @pl.when(there & (rw > 0))
        def _():
            one(0)

        @pl.when(there & (rw < n_rw - 1))
        def _():
            one(rows + 1)

        @pl.when(jnp.logical_not(there))
        def _():
            xn[e] = jnp.zeros_like(xn[e])

        @pl.when(there & (rw == 0))
        def _():
            nothing(0)

        @pl.when(there & (rw == n_rw - 1))
        def _():
            nothing(rows + 1)

    def time_taps(w, v):
        for a in range(3):
            outer = (w[a * 3].astype(jnp.float32) + w[a * 3 + 2].astype(jnp.float32)) * 0.5
            inner = w[a * 3 + 1].astype(jnp.float32) * 0.5
            v[a] = (outer - inner).astype(jnp.bfloat16)
            w[a * 3 + 1] = (outer + inner).astype(jnp.bfloat16)

    def frame(e):
        return xn[e].astype(jnp.float32)

    col = lax.broadcasted_iota(jnp.int32, (pix, chans), 0) % cols

    def product(w, v, k, e):
        total = None
        for a in range(3):
            tap = (w.at[a * 3], w.at[a * 3 + 1], v.at[a], w.at[a * 3 + 2])[k]
            part = jnp.dot(un[k, a * cols:a * cols + pix, :], tap[:, e * chans:(e + 1) * chans],
                           preferred_element_type=jnp.float32)
            total = part if total is None else total + part
        return total

    def column(y, e):
        if e == 0:
            return jnp.where(col == 0, 0.0, pltpu.roll(y, 1, 0))
        if e == 2:
            return jnp.where(col == cols - 1, 0.0, pltpu.roll(y, pix - 1, 0))
        return y

    def conv_late(w, v, f, bias):
        d1, d2, d3 = frame(f + 1), frame(f + 2), frame(f + 3)
        un[1] = (d1 + d2).astype(jnp.bfloat16)
        un[2] = (d2 - d1).astype(jnp.bfloat16)
        un[3] = (d1 - d3).astype(jnp.bfloat16)
        y0 = y1 = bias
        for e in (1, 0, 2):
            m1, m2, m3 = [product(w, v, k, e) for k in (1, 2, 3)]
            y0, y1 = y0 + column(m1 + m2, e), y1 + column(m1 - m2 - m3, e)
        acc[...] = y0
        return y1

    def conv_early(w, v, f):
        un[0] = (frame(f) - frame(f + 2)).astype(jnp.bfloat16)
        y = acc[...]
        for e in (1, 0, 2):
            y = y + column(product(w, v, 0, e), e)
        return y

    stats_start(0)
    halo_start(fx, 0, EDGES, 1)
    long_start(fx, 0, 0)
    halo_start(fx, 0, EDGES, 0)
    halo_start(fx, 0, MIDDLE, 1)
    halo_start(fx, 0, MIDDLE[:1], 0)
    for e in range(2, 2 + frames):
        halo_start(fx, 0, ROW, e)
    for c in small:
        c.wait()
    for c in taps[:3]:
        c.wait()
    time_taps(wa, va)

    def rest_first():
        for c in taps[3:]:
            c.wait()
        time_taps(wb, vb)
        long_start(fx, 0, 1)

    def edges_on(buf, n, e):
        halo_here(buf, n, EDGES, e)
        halo_edge(buf, n, e)

    stats_finish(0, par[0], par[1], rest_first)
    for e in range(2, 2 + frames):
        halo_here(fx, 0, ROW, e)
        normalise(fx, e)
    edges_on(fx, 0, 1)
    long_start(fx, 0, 2)

    def earlier(buf, n, i, e):
        @pl.when(i == 1)
        def _():
            halo_here(buf, n, MIDDLE, e)
            halo_corner(buf, n, e)
            normalise(buf, e)

    def first_conv(i, _):
        f = 2 - 2 * i

        def put(g, y):
            y = y.astype(jnp.bfloat16)
            bx[2 + g, 1:rows + 1] = y.reshape(rows, cols, chans)
            put_sums(1, g, *frame_sums(y.astype(jnp.float32)))
            halo_start(bx, 1, ROW, 2 + g)

        earlier(fx, 0, i, 1)
        put(f + 1, conv_late(wa, va, f, par[2]))

        @pl.when(i == 0)
        def _():
            halo_start(bx, 1, EDGES, 1)
            long_start(bx, 1, 0)
            edges_on(fx, 0, 0)

        @pl.when(i == 1)
        def _():
            long_start(bx, 1, 1)

        earlier(fx, 0, i, 0)
        put(f, conv_early(wa, va, f))
        return 0

    lax.fori_loop(0, 2, first_conv, 0)

    stats_start(1)
    halo_start(bx, 1, EDGES, 0)
    halo_start(bx, 1, MIDDLE[:1], 1)
    halo_start(bx, 1, MIDDLE, 0)
    stats_finish(1, par[3], par[4], lambda: long_start(bx, 1, 2))
    edges_on(bx, 1, 1)
    for e in range(2, 2 + frames):
        halo_here(bx, 1, ROW, e)
        normalise(bx, e)

    def second_conv(i, _):
        f = 2 - 2 * i

        def put(g, y):
            y = y + fx[2 + g, 1:rows + 1].reshape(pix, chans).astype(jnp.float32)
            out[g] = y.astype(jnp.bfloat16).reshape(rows, cols, chans)

        earlier(bx, 1, i, 1)
        put(f + 1, conv_late(wb, vb, f, par[5]))

        @pl.when(i == 0)
        def _():
            edges_on(bx, 1, 0)

        earlier(bx, 1, i, 0)
        put(f, conv_early(wb, vb, f))
        return 0

    lax.fori_loop(0, 2, second_conv, 0)

    for n, buf in enumerate((fx, bx)):
        for e in (1, 0):
            halo_sent(buf, n, [kind for kind in TIME if (kind, e) != LONG[n]], e)

            @pl.when(tm > 0)
            def _():
                halo_sent(buf, n, ROW, e)
        for e in range(2, 2 + frames):
            halo_sent(buf, n, ROW, e)
        stats_sent(n)
        long_sent(buf, n)


def solution(mesh):
    n_tm, n_rw = mesh.shape["tm"], mesh.shape["rows"]

    def on_device(features, gamma_one, beta_one, weight_one, bias_one, gamma_two, beta_two, weight_two, bias_two):
        frames, rows, cols, chans = features.shape
        taps = lambda w: w.reshape(9, 3, chans, chans)
        line = lambda v: v.reshape(1, chans)
        bf16, f32 = jnp.bfloat16, jnp.float32
        dma = pltpu.SemaphoreType.DMA
        return pl.pallas_call(
            functools.partial(block_kernel, n_tm, n_rw, frames, rows, cols, chans),
            out_shape=jax.ShapeDtypeStruct(features.shape, bf16),
            in_specs=[HBM] * 9,
            out_specs=pl.BlockSpec(memory_space=pltpu.VMEM),
            scratch_shapes=[
                pltpu.VMEM((frames + 2, rows + 2, cols, chans), bf16),
                pltpu.VMEM((frames + 2, rows + 2, cols, chans), bf16),
                pltpu.VMEM((frames + 2, (rows + 2) * cols, chans), bf16),
                pltpu.VMEM((4, (rows + 2) * cols, chans), bf16),
                pltpu.VMEM((rows * cols, chans), f32),
                pltpu.VMEM((9, chans, 3 * chans), bf16),
                pltpu.VMEM((9, chans, 3 * chans), bf16),
                pltpu.VMEM((3, chans, 3 * chans), bf16),
                pltpu.VMEM((3, chans, 3 * chans), bf16),
                pltpu.VMEM((6, 1, chans), f32),
                pltpu.VMEM((2, 2 * frames, chans), f32),
                pltpu.VMEM((2, 1, chans), f32),
                pltpu.VMEM((2, 3, 1, chans), f32),
                pltpu.VMEM((2, n_rw - 1, 3, 1, chans), f32),
                pltpu.VMEM((2, n_tm - 1, 1, chans), f32),
                pltpu.VMEM((3, 8, chans), f32),
                pltpu.VMEM((2, 2, rows // 4, cols, chans), bf16),
                dma((frames,)), dma((6,)), dma((2, 3)),
                dma((2,)), dma((2,)), dma((2,)), dma((2,)),
                dma((2, 6, frames + 2)), dma((2, 6, frames + 2)), dma((2, 3)), dma((2, 2)),
            ],
            compiler_params=pltpu.CompilerParams(
                collective_id=0, has_side_effects=True, vmem_limit_bytes=52 << 20),
        )(*[pltpu.with_memory_space_constraint(v, pltpu.HBM) for v in (
            features, line(gamma_one), line(beta_one), taps(weight_one), line(bias_one),
            line(gamma_two), line(beta_two), taps(weight_two), line(bias_two))])

    placed = (P("tm", "rows", None, None), P(), P(), P(), P(), P(), P(), P(), P())
    return jax.shard_map(on_device, mesh=mesh, in_specs=placed, out_specs=P("tm", "rows", None, None), check_vma=False)
```

```python
import functools

import jax
import jax.numpy as jnp
from jax import lax
from jax.experimental import pallas as pl
from jax.experimental.pallas import tpu as pltpu
from jax.sharding import PartitionSpec as P

MESH = pl.DeviceIdType.MESH
GROUPS = 32
EPSILON = 1e-06
RING = 4
HBM = pl.BlockSpec(memory_space=pltpu.HBM)


def group_sum(x, per_group):
    lane = lax.broadcasted_iota(jnp.int32, x.shape, 1)
    step = 1
    while step < per_group:
        up = pltpu.roll(x, x.shape[1] - step, 1)
        down = pltpu.roll(x, step, 1)
        x = x + jnp.where((lane & step) == 0, up, down)
        step *= 2
    return x


def block_kernel(n_tm, n_rw, frames, rows, cols, chans,
                 feat, g1, b1, w1, c1, g2, b2, w2, c2, out,
                 fx, bx, xn, un, acc, wa, wb, va, vb, par, sl, ln, lt, ra, tb, st, rel,
                 lsem, psem, wsem, rsend, rrecv, tsend, trecv, hsend, hrecv, gsend, grecv):
    tm = lax.axis_index("tm")
    rw = lax.axis_index("rows")
    pix = rows * cols
    per_group = chans // GROUPS

    loads = [pltpu.make_async_copy(feat.at[f], fx.at[2 + f, 1:rows + 1], lsem.at[f]) for f in range(frames)]
    for c in loads:
        c.start()
    small = [pltpu.make_async_copy(p, par.at[i], psem.at[i]) for i, p in enumerate((g1, b1, c1, g2, b2, c2))]
    for c in small:
        c.start()
    taps = [
        pltpu.make_async_copy(w.at[:, e], v.at[:, :, e * chans:(e + 1) * chans], wsem.at[n, e])
        for n, (w, v) in enumerate(((w1, wa), (w2, wb))) for e in range(3)
    ]
    for c in taps:
        c.start()

    barrier = pltpu.get_barrier_semaphore()
    for k in range(1, n_rw):
        pl.semaphore_signal(barrier, 1, device_id=(tm, lax.rem(rw + k, n_rw)), device_id_type=MESH)
    for k in range(1, n_tm):
        pl.semaphore_signal(barrier, 1, device_id=(lax.rem(tm + k, n_tm), rw), device_id_type=MESH)

    def frame_sums(z):
        part1 = jnp.sum(z.reshape(z.shape[0] // 8, 8, chans), axis=0)
        part2 = jnp.sum((z * z).reshape(z.shape[0] // 8, 8, chans), axis=0)
        return part1, part2

    def put_sums(which, f, part1, part2):
        sl[which, pl.ds(f, 1), :] = jnp.sum(part1, axis=0, keepdims=True)
        sl[which, pl.ds(frames + f, 1), :] = jnp.sum(part2, axis=0, keepdims=True)

    for f in range(frames):
        loads[f].wait()

        def add_row(r, carry, f=f):
            one, two = frame_sums(fx[2 + f, pl.ds(1 + 8 * r, 8)].reshape(8 * cols, chans).astype(jnp.float32))
            return carry[0] + one, carry[1] + two

        zero = jnp.zeros((8, chans), jnp.float32)
        one, two = lax.fori_loop(0, rows // 8, add_row, (zero, zero))
        put_sums(0, f, one, two)

    pl.semaphore_wait(barrier, n_rw - 1 + n_tm - 1)

    quarter = rows // 4

    def halo(buf, n, kind, e):
        def remote(src, dst, dev):
            return pltpu.make_async_remote_copy(
                src_ref=src, dst_ref=dst, send_sem=hsend.at[n, kind, e], recv_sem=hrecv.at[n, kind, e],
                device_id=dev, device_id_type=MESH)
        if kind == 0:
            return remote(buf.at[e, rows], buf.at[e, 0], (tm, rw + 1))
        if kind == 1:
            return remote(buf.at[e, 1], buf.at[e, rows + 1], (tm, rw - 1))
        part = pl.ds(1 + (kind - 2) * quarter, quarter)
        return remote(buf.at[e + frames, part], buf.at[e, part], (tm + 1, rw))

    ROW, TIME, EDGES, MIDDLE = (0, 1), (2, 3, 4, 5), (2, 5), (3, 4)
    sends = ((rw < n_rw - 1), (rw > 0)) + (tm < n_tm - 1,) * 4
    gets = ((rw > 0), (rw < n_rw - 1)) + (tm > 0,) * 4

    def halo_start(buf, n, kinds, e):
        for kind in kinds:
            @pl.when(sends[kind])
            def _():
                halo(buf, n, kind, e).start()

    def halo_sent(buf, n, kinds, e):
        for kind in kinds:
            @pl.when(sends[kind])
            def _():
                halo(buf, n, kind, e).wait_send()

    def halo_here(buf, n, kinds, e):
        for kind in kinds:
            @pl.when(gets[kind])
            def _():
                halo(buf, n, kind, e).wait_recv()

    LONG = ((4, 0), (4, 1))

    def ring(step):
        return tm - lax.rem(tm, RING) + lax.rem(tm + step, RING)

    def long_copy(buf, n, hop):
        kind, e = LONG[n]
        part = pl.ds(1 + (kind - 2) * quarter, quarter)
        src = (buf.at[e + frames, part], rel.at[n, 0], rel.at[n, 1])[hop]
        dst = (rel.at[n, 0], rel.at[n, 1], buf.at[e, part])[hop]
        return pltpu.make_async_remote_copy(
            src_ref=src, dst_ref=dst, send_sem=gsend.at[n, hop],
            recv_sem=hrecv.at[n, kind, e] if hop == 2 else grecv.at[n, hop],
            device_id=(ring(2) + 1 if hop == 2 else ring(RING - 1), rw), device_id_type=MESH)

    def long_start(buf, n, hop):
        @pl.when(ring(hop) < n_tm - 1)
        def _():
            if hop:
                long_copy(buf, n, hop - 1).wait_recv()
            long_copy(buf, n, hop).start()

    def long_sent(buf, n):
        for hop in range(3):
            @pl.when(ring(hop) < n_tm - 1)
            def _():
                long_copy(buf, n, hop).wait_send()

    def halo_edge(buf, n, e):
        @pl.when(tm > 0)
        def _():
            halo_start(buf, n, ROW, e)

    def halo_corner(buf, n, e):
        @pl.when(tm > 0)
        def _():
            halo_here(buf, n, ROW, e)

    place = lax.broadcasted_iota(jnp.int32, (2 * frames, chans), 0)
    keep = (lax.broadcasted_iota(jnp.int32, (2 * frames, chans), 1) % per_group) == place

    def pack(x):
        return jnp.sum(jnp.where(keep, group_sum(x, per_group), 0.0), axis=0, keepdims=True)

    def unpack(line):
        return group_sum(jnp.where(keep, line, 0.0), per_group)

    def row_copy(n, k):
        return pltpu.make_async_remote_copy(
            src_ref=lt.at[n], dst_ref=ra.at[n, k - 1], send_sem=rsend.at[n], recv_sem=rrecv.at[n],
            device_id=(tm, lax.rem(rw + k, n_rw)), device_id_type=MESH)

    def time_copy(n, k):
        return pltpu.make_async_remote_copy(
            src_ref=ln.at[n], dst_ref=tb.at[n, k - 1], send_sem=tsend.at[n], recv_sem=trecv.at[n],
            device_id=(lax.rem(tm + k, n_tm), rw), device_id_type=MESH)

    def all_rows(n):
        return pltpu.make_async_remote_copy(
            src_ref=ra.at[n], dst_ref=ra.at[n], send_sem=rsend.at[n], recv_sem=rrecv.at[n],
            device_id=(tm, lax.rem(rw + 1, n_rw)), device_id_type=MESH)

    def all_times(n):
        return pltpu.make_async_remote_copy(
            src_ref=tb.at[n], dst_ref=tb.at[n], send_sem=tsend.at[n], recv_sem=trecv.at[n],
            device_id=(lax.rem(tm + 1, n_tm), rw), device_id_type=MESH)

    def stats_start(n):
        ln[n] = pack(sl[n])
        for k in (10, 6, 9, 11, 14, 2, 5, 7, 8, 12, 13, 15, 3, 4, 1):
            time_copy(n, k).start()

    def stats_finish(n, gain, shift, meanwhile):
        all_times(n).wait_recv()
        ago = lax.broadcasted_iota(jnp.int32, (n_tm - 1, 1, chans), 0) + 1
        times = jnp.where(ago <= tm, tb[n], 0.0)
        lt[n, 0] = jnp.sum(times[1:], axis=0)
        lt[n, 1] = times[0]
        lt[n, 2] = ln[n]
        for k in (4, 5, 3, 2, 6, 7, 1):
            row_copy(n, k).start()
        meanwhile()
        all_rows(n).wait_recv()
        lines = lt[n] + jnp.sum(ra[n], axis=0)
        far, near, mine = unpack(lines[0]), unpack(lines[1]), unpack(lines[2])

        def running(lo):
            total = jnp.sum(far[lo:lo + frames], axis=0, keepdims=True)
            for f in range(frames - 1):
                total = total + near[lo + f:lo + f + 1]
            result = [total]
            total = total + near[lo + frames - 1:lo + frames]
            result.append(total)
            for f in range(frames):
                total = total + mine[lo + f:lo + f + 1]
                result.append(total)
            pad = jnp.zeros((8 - len(result), chans), jnp.float32)
            return jnp.concatenate(result + [pad], axis=0)

        one, two = running(0), running(frames)
        count = jnp.maximum(tm * frames + place - 1, 1).astype(jnp.float32) * float(n_rw * pix * per_group)
        mean = one / count
        var = two / count - mean * mean
        st[0] = mean
        st[1] = lax.rsqrt(var + EPSILON) * (0.5 * gain)
        st[2, 0:1] = 0.5 * shift

    def stats_sent(n):
        all_rows(n).wait_send()
        all_times(n).wait_send()

    def normalise(buf, e):
        mean, scale, shift = st[0, pl.ds(e, 1), :], st[1, pl.ds(e, 1), :], st[2, 0:1]

        def one(r):
            half = (buf[e, r].astype(jnp.float32) - mean) * scale + shift
            xn[e, pl.ds(pl.multiple_of(r * cols, cols), cols), :] = (half + half * jnp.tanh(half)).astype(jnp.bfloat16)

        def nothing(r):
            xn[e, pl.ds(r * cols, cols), :] = jnp.zeros((cols, chans), jnp.bfloat16)

        there = (tm > 0) | (e >= 2)

        @pl.when(there)
        def _():
            def eight(i, _):
                for r in range(1, 9):
                    one(r + 8 * i)
                return 0
            lax.fori_loop(0, rows // 8, eight, 0)

        @pl.when(there & (rw > 0))
        def _():
            one(0)

        @pl.when(there & (rw < n_rw - 1))
        def _():
            one(rows + 1)

        @pl.when(jnp.logical_not(there))
        def _():
            xn[e] = jnp.zeros_like(xn[e])

        @pl.when(there & (rw == 0))
        def _():
            nothing(0)

        @pl.when(there & (rw == n_rw - 1))
        def _():
            nothing(rows + 1)

    def time_taps(w, v):
        for a in range(3):
            outer = (w[a * 3].astype(jnp.float32) + w[a * 3 + 2].astype(jnp.float32)) * 0.5
            inner = w[a * 3 + 1].astype(jnp.float32) * 0.5
            v[a] = (outer - inner).astype(jnp.bfloat16)
            w[a * 3 + 1] = (outer + inner).astype(jnp.bfloat16)

    def frame(e):
        return xn[e].astype(jnp.float32)

    half_pix = pix // 2
    col = lax.broadcasted_iota(jnp.int32, (half_pix, chans), 0) % cols

    def product(w, v, k, e, at):
        total = None
        for a in range(3):
            tap = (w.at[a * 3], w.at[a * 3 + 1], v.at[a], w.at[a * 3 + 2])[k]
            part = jnp.dot(un[k, at + a * cols:at + a * cols + half_pix, :], tap[:, e * chans:(e + 1) * chans],
                           preferred_element_type=jnp.float32)
            total = part if total is None else total + part
        return total

    def column(y, e):
        if e == 0:
            return jnp.where(col == 0, 0.0, pltpu.roll(y, 1, 0))
        if e == 2:
            return jnp.where(col == cols - 1, 0.0, pltpu.roll(y, half_pix - 1, 0))
        return y

    def conv_late(w, v, f, bias):
        d1, d2, d3 = frame(f + 1), frame(f + 2), frame(f + 3)
        un[1] = (d1 + d2).astype(jnp.bfloat16)
        un[2] = (d2 - d1).astype(jnp.bfloat16)
        un[3] = (d1 - d3).astype(jnp.bfloat16)
        parts = []
        for at in (0, half_pix):
            y0 = y1 = bias
            for e in (1, 0, 2):
                m1, m2, m3 = [product(w, v, k, e, at) for k in (1, 2, 3)]
                y0, y1 = y0 + column(m1 + m2, e), y1 + column(m1 - m2 - m3, e)
            acc[at:at + half_pix] = y0
            parts.append(y1)
        return jnp.concatenate(parts, axis=0)

    def conv_early(w, v, f):
        un[0] = (frame(f) - frame(f + 2)).astype(jnp.bfloat16)
        parts = []
        for at in (0, half_pix):
            y = acc[at:at + half_pix]
            for e in (1, 0, 2):
                y = y + column(product(w, v, 0, e, at), e)
            parts.append(y)
        return jnp.concatenate(parts, axis=0)

    stats_start(0)
    halo_start(fx, 0, EDGES, 1)
    long_start(fx, 0, 0)
    halo_start(fx, 0, EDGES, 0)
    halo_start(fx, 0, MIDDLE, 1)
    halo_start(fx, 0, MIDDLE[:1], 0)
    for e in range(2, 2 + frames):
        halo_start(fx, 0, ROW, e)
    for c in small:
        c.wait()
    for c in taps[:3]:
        c.wait()
    time_taps(wa, va)

    def rest_first():
        for c in taps[3:]:
            c.wait()
        time_taps(wb, vb)
        long_start(fx, 0, 1)

    def edges_on(buf, n, e):
        halo_here(buf, n, EDGES, e)
        halo_edge(buf, n, e)

    stats_finish(0, par[0], par[1], rest_first)
    for e in range(2, 2 + frames):
        halo_here(fx, 0, ROW, e)
        normalise(fx, e)
    edges_on(fx, 0, 1)
    long_start(fx, 0, 2)

    def earlier(buf, n, i, e):
        @pl.when(i == 1)
        def _():
            halo_here(buf, n, MIDDLE, e)
            halo_corner(buf, n, e)
            normalise(buf, e)

    def first_conv(i, _):
        f = 2 - 2 * i

        def put(g, y):
            y = y.astype(jnp.bfloat16)
            bx[2 + g, 1:rows + 1] = y.reshape(rows, cols, chans)
            put_sums(1, g, *frame_sums(y.astype(jnp.float32)))
            halo_start(bx, 1, ROW, 2 + g)

        earlier(fx, 0, i, 1)
        put(f + 1, conv_late(wa, va, f, par[2]))

        @pl.when(i == 0)
        def _():
            long_start(bx, 1, 0)
            edges_on(fx, 0, 0)

        @pl.when(i == 1)
        def _():
            long_start(bx, 1, 1)

        earlier(fx, 0, i, 0)
        put(f, conv_early(wa, va, f))
        return 0

    lax.fori_loop(0, 2, first_conv, 0)

    stats_start(1)
    halo_start(bx, 1, EDGES, 1)
    halo_start(bx, 1, EDGES, 0)
    halo_start(bx, 1, MIDDLE[:1], 1)
    halo_start(bx, 1, MIDDLE, 0)
    stats_finish(1, par[3], par[4], lambda: long_start(bx, 1, 2))
    edges_on(bx, 1, 1)
    for e in range(2, 2 + frames):
        halo_here(bx, 1, ROW, e)
        normalise(bx, e)

    def second_conv(i, _):
        f = 2 - 2 * i

        def put(g, y):
            y = y + fx[2 + g, 1:rows + 1].reshape(pix, chans).astype(jnp.float32)
            out[g] = y.astype(jnp.bfloat16).reshape(rows, cols, chans)

        earlier(bx, 1, i, 1)
        put(f + 1, conv_late(wb, vb, f, par[5]))

        @pl.when(i == 0)
        def _():
            edges_on(bx, 1, 0)

        earlier(bx, 1, i, 0)
        put(f, conv_early(wb, vb, f))
        return 0

    lax.fori_loop(0, 2, second_conv, 0)

    for n, buf in enumerate((fx, bx)):
        for e in (1, 0):
            halo_sent(buf, n, [kind for kind in TIME if (kind, e) != LONG[n]], e)

            @pl.when(tm > 0)
            def _():
                halo_sent(buf, n, ROW, e)
        for e in range(2, 2 + frames):
            halo_sent(buf, n, ROW, e)
        stats_sent(n)
        long_sent(buf, n)


def solution(mesh):
    n_tm, n_rw = mesh.shape["tm"], mesh.shape["rows"]

    def on_device(features, gamma_one, beta_one, weight_one, bias_one, gamma_two, beta_two, weight_two, bias_two):
        frames, rows, cols, chans = features.shape
        taps = lambda w: w.reshape(9, 3, chans, chans)
        line = lambda v: v.reshape(1, chans)
        bf16, f32 = jnp.bfloat16, jnp.float32
        dma = pltpu.SemaphoreType.DMA
        return pl.pallas_call(
            functools.partial(block_kernel, n_tm, n_rw, frames, rows, cols, chans),
            out_shape=jax.ShapeDtypeStruct(features.shape, bf16),
            in_specs=[HBM] * 9,
            out_specs=pl.BlockSpec(memory_space=pltpu.VMEM),
            scratch_shapes=[
                pltpu.VMEM((frames + 2, rows + 2, cols, chans), bf16),
                pltpu.VMEM((frames + 2, rows + 2, cols, chans), bf16),
                pltpu.VMEM((frames + 2, (rows + 2) * cols, chans), bf16),
                pltpu.VMEM((4, (rows + 2) * cols, chans), bf16),
                pltpu.VMEM((rows * cols, chans), f32),
                pltpu.VMEM((9, chans, 3 * chans), bf16),
                pltpu.VMEM((9, chans, 3 * chans), bf16),
                pltpu.VMEM((3, chans, 3 * chans), bf16),
                pltpu.VMEM((3, chans, 3 * chans), bf16),
                pltpu.VMEM((6, 1, chans), f32),
                pltpu.VMEM((2, 2 * frames, chans), f32),
                pltpu.VMEM((2, 1, chans), f32),
                pltpu.VMEM((2, 3, 1, chans), f32),
                pltpu.VMEM((2, n_rw - 1, 3, 1, chans), f32),
                pltpu.VMEM((2, n_tm - 1, 1, chans), f32),
                pltpu.VMEM((3, 8, chans), f32),
                pltpu.VMEM((2, 2, rows // 4, cols, chans), bf16),
                dma((frames,)), dma((6,)), dma((2, 3)),
                dma((2,)), dma((2,)), dma((2,)), dma((2,)),
                dma((2, 6, frames + 2)), dma((2, 6, frames + 2)), dma((2, 3)), dma((2, 2)),
            ],
            compiler_params=pltpu.CompilerParams(
                collective_id=0, has_side_effects=True, vmem_limit_bytes=52 << 20),
        )(*[pltpu.with_memory_space_constraint(v, pltpu.HBM) for v in (
            features, line(gamma_one), line(beta_one), taps(weight_one), line(bias_one),
            line(gamma_two), line(beta_two), taps(weight_two), line(bias_two))])

    placed = (P("tm", "rows", None, None), P(), P(), P(), P(), P(), P(), P(), P())
    return jax.shard_map(on_device, mesh=mesh, in_specs=placed, out_specs=P("tm", "rows", None, None), check_vma=False)
```

```python
import functools

import jax
import jax.numpy as jnp
from jax import lax
from jax.experimental import pallas as pl
from jax.experimental.pallas import tpu as pltpu
from jax.sharding import PartitionSpec as P

MESH = pl.DeviceIdType.MESH
GROUPS = 32
EPSILON = 1e-06
RING = 4
HBM = pl.BlockSpec(memory_space=pltpu.HBM)


def group_sum(x, per_group):
    lane = lax.broadcasted_iota(jnp.int32, x.shape, 1)
    step = 1
    while step < per_group:
        up = pltpu.roll(x, x.shape[1] - step, 1)
        down = pltpu.roll(x, step, 1)
        x = x + jnp.where((lane & step) == 0, up, down)
        step *= 2
    return x


def block_kernel(n_tm, n_rw, frames, rows, cols, chans,
                 feat, g1, b1, w1, c1, g2, b2, w2, c2, out,
                 fx, bx, xn, un, acc, wa, wb, va, vb, par, sl, ln, lt, ra, tb, st, rel,
                 lsem, psem, wsem, rsend, rrecv, tsend, trecv, hsend, hrecv, gsend, grecv):
    tm = lax.axis_index("tm")
    rw = lax.axis_index("rows")
    pix = rows * cols
    per_group = chans // GROUPS

    loads = [pltpu.make_async_copy(feat.at[f], fx.at[2 + f, 1:rows + 1], lsem.at[f]) for f in range(frames)]
    for c in loads:
        c.start()
    small = [pltpu.make_async_copy(p, par.at[i], psem.at[i]) for i, p in enumerate((g1, b1, c1, g2, b2, c2))]
    for c in small:
        c.start()
    taps = [
        pltpu.make_async_copy(w.at[:, e], v.at[:, :, e * chans:(e + 1) * chans], wsem.at[n, e])
        for n, (w, v) in enumerate(((w1, wa), (w2, wb))) for e in range(3)
    ]
    for c in taps:
        c.start()

    barrier = pltpu.get_barrier_semaphore()
    for k in range(1, n_rw):
        pl.semaphore_signal(barrier, 1, device_id=(tm, lax.rem(rw + k, n_rw)), device_id_type=MESH)
    for k in range(1, n_tm):
        pl.semaphore_signal(barrier, 1, device_id=(lax.rem(tm + k, n_tm), rw), device_id_type=MESH)

    def frame_sums(z):
        part1 = jnp.sum(z.reshape(z.shape[0] // 8, 8, chans), axis=0)
        part2 = jnp.sum((z * z).reshape(z.shape[0] // 8, 8, chans), axis=0)
        return part1, part2

    def put_sums(which, f, part1, part2):
        sl[which, pl.ds(f, 1), :] = jnp.sum(part1, axis=0, keepdims=True)
        sl[which, pl.ds(frames + f, 1), :] = jnp.sum(part2, axis=0, keepdims=True)

    for f in range(frames):
        loads[f].wait()

        def add_row(r, carry, f=f):
            one, two = frame_sums(fx[2 + f, pl.ds(1 + 8 * r, 8)].reshape(8 * cols, chans).astype(jnp.float32))
            return carry[0] + one, carry[1] + two

        zero = jnp.zeros((8, chans), jnp.float32)
        one, two = lax.fori_loop(0, rows // 8, add_row, (zero, zero))
        put_sums(0, f, one, two)

    pl.semaphore_wait(barrier, n_rw - 1 + n_tm - 1)

    quarter = rows // 4

    def halo(buf, n, kind, e):
        def remote(src, dst, dev):
            return pltpu.make_async_remote_copy(
                src_ref=src, dst_ref=dst, send_sem=hsend.at[n, kind, e], recv_sem=hrecv.at[n, kind, e],
                device_id=dev, device_id_type=MESH)
        if kind == 0:
            return remote(buf.at[e, rows], buf.at[e, 0], (tm, rw + 1))
        if kind == 1:
            return remote(buf.at[e, 1], buf.at[e, rows + 1], (tm, rw - 1))
        part = pl.ds(1 + (kind - 2) * quarter, quarter)
        return remote(buf.at[e + frames, part], buf.at[e, part], (tm + 1, rw))

    ROW, TIME, EDGES, MIDDLE = (0, 1), (2, 3, 4, 5), (2, 5), (3, 4)
    sends = ((rw < n_rw - 1), (rw > 0)) + (tm < n_tm - 1,) * 4
    gets = ((rw > 0), (rw < n_rw - 1)) + (tm > 0,) * 4

    def halo_start(buf, n, kinds, e):
        for kind in kinds:
            @pl.when(sends[kind])
            def _():
                halo(buf, n, kind, e).start()

    def halo_sent(buf, n, kinds, e):
        for kind in kinds:
            @pl.when(sends[kind])
            def _():
                halo(buf, n, kind, e).wait_send()

    def halo_here(buf, n, kinds, e):
        for kind in kinds:
            @pl.when(gets[kind])
            def _():
                halo(buf, n, kind, e).wait_recv()

    LONG = ((4, 0), (4, 1))

    def ring(step):
        return tm - lax.rem(tm, RING) + lax.rem(tm + step, RING)

    def long_copy(buf, n, hop):
        kind, e = LONG[n]
        part = pl.ds(1 + (kind - 2) * quarter, quarter)
        src = (buf.at[e + frames, part], rel.at[n, 0], rel.at[n, 1])[hop]
        dst = (rel.at[n, 0], rel.at[n, 1], buf.at[e, part])[hop]
        return pltpu.make_async_remote_copy(
            src_ref=src, dst_ref=dst, send_sem=gsend.at[n, hop],
            recv_sem=hrecv.at[n, kind, e] if hop == 2 else grecv.at[n, hop],
            device_id=(ring(2) + 1 if hop == 2 else ring(RING - 1), rw), device_id_type=MESH)

    def long_start(buf, n, hop):
        @pl.when(ring(hop) < n_tm - 1)
        def _():
            if hop:
                long_copy(buf, n, hop - 1).wait_recv()
            long_copy(buf, n, hop).start()

    def long_sent(buf, n):
        for hop in range(3):
            @pl.when(ring(hop) < n_tm - 1)
            def _():
                long_copy(buf, n, hop).wait_send()

    def halo_edge(buf, n, e):
        @pl.when(tm > 0)
        def _():
            halo_start(buf, n, ROW, e)

    def halo_corner(buf, n, e):
        @pl.when(tm > 0)
        def _():
            halo_here(buf, n, ROW, e)

    place = lax.broadcasted_iota(jnp.int32, (2 * frames, chans), 0)
    keep = (lax.broadcasted_iota(jnp.int32, (2 * frames, chans), 1) % per_group) == place

    def pack(x):
        return jnp.sum(jnp.where(keep, group_sum(x, per_group), 0.0), axis=0, keepdims=True)

    def unpack(line):
        return group_sum(jnp.where(keep, line, 0.0), per_group)

    def row_copy(n, k):
        return pltpu.make_async_remote_copy(
            src_ref=lt.at[n], dst_ref=ra.at[n, k - 1], send_sem=rsend.at[n], recv_sem=rrecv.at[n],
            device_id=(tm, lax.rem(rw + k, n_rw)), device_id_type=MESH)

    def time_copy(n, k):
        return pltpu.make_async_remote_copy(
            src_ref=ln.at[n], dst_ref=tb.at[n, k - 1], send_sem=tsend.at[n], recv_sem=trecv.at[n],
            device_id=(lax.rem(tm + k, n_tm), rw), device_id_type=MESH)

    def all_rows(n):
        return pltpu.make_async_remote_copy(
            src_ref=ra.at[n], dst_ref=ra.at[n], send_sem=rsend.at[n], recv_sem=rrecv.at[n],
            device_id=(tm, lax.rem(rw + 1, n_rw)), device_id_type=MESH)

    def all_times(n):
        return pltpu.make_async_remote_copy(
            src_ref=tb.at[n], dst_ref=tb.at[n], send_sem=tsend.at[n], recv_sem=trecv.at[n],
            device_id=(lax.rem(tm + 1, n_tm), rw), device_id_type=MESH)

    def stats_start(n):
        ln[n] = pack(sl[n])
        for k in (10, 6, 9, 11, 14, 2, 5, 7, 8, 12, 13, 15, 3, 4, 1):
            time_copy(n, k).start()

    def stats_finish(n, gain, shift, meanwhile):
        all_times(n).wait_recv()
        ago = lax.broadcasted_iota(jnp.int32, (n_tm - 1, 1, chans), 0) + 1
        times = jnp.where(ago <= tm, tb[n], 0.0)
        lt[n, 0] = jnp.sum(times[1:], axis=0)
        lt[n, 1] = times[0]
        lt[n, 2] = ln[n]
        for k in (4, 5, 3, 2, 6, 7, 1):
            row_copy(n, k).start()
        meanwhile()
        all_rows(n).wait_recv()
        lines = lt[n] + jnp.sum(ra[n], axis=0)
        far, near, mine = unpack(lines[0]), unpack(lines[1]), unpack(lines[2])

        def running(lo):
            total = jnp.sum(far[lo:lo + frames], axis=0, keepdims=True)
            for f in range(frames - 1):
                total = total + near[lo + f:lo + f + 1]
            result = [total]
            total = total + near[lo + frames - 1:lo + frames]
            result.append(total)
            for f in range(frames):
                total = total + mine[lo + f:lo + f + 1]
                result.append(total)
            pad = jnp.zeros((8 - len(result), chans), jnp.float32)
            return jnp.concatenate(result + [pad], axis=0)

        one, two = running(0), running(frames)
        count = jnp.maximum(tm * frames + place - 1, 1).astype(jnp.float32) * float(n_rw * pix * per_group)
        mean = one / count
        var = two / count - mean * mean
        st[0] = mean
        st[1] = lax.rsqrt(var + EPSILON) * (0.5 * gain)
        st[2, 0:1] = 0.5 * shift

    def stats_sent(n):
        all_rows(n).wait_send()
        all_times(n).wait_send()

    def normalise(buf, e):
        mean, scale, shift = st[0, pl.ds(e, 1), :], st[1, pl.ds(e, 1), :], st[2, 0:1]

        def one(r):
            half = (buf[e, r].astype(jnp.float32) - mean) * scale + shift
            xn[e, pl.ds(pl.multiple_of(r * cols, cols), cols), :] = (half + half * jnp.tanh(half)).astype(jnp.bfloat16)

        def nothing(r):
            xn[e, pl.ds(r * cols, cols), :] = jnp.zeros((cols, chans), jnp.bfloat16)

        there = (tm > 0) | (e >= 2)

        @pl.when(there)
        def _():
            def eight(i, _):
                for r in range(1, 9):
                    one(r + 8 * i)
                return 0
            lax.fori_loop(0, rows // 8, eight, 0)

        @pl.when(there & (rw > 0))
        def _():
            one(0)

        @pl.when(there & (rw < n_rw - 1))
        def _():
            one(rows + 1)

        @pl.when(jnp.logical_not(there))
        def _():
            xn[e] = jnp.zeros_like(xn[e])

        @pl.when(there & (rw == 0))
        def _():
            nothing(0)

        @pl.when(there & (rw == n_rw - 1))
        def _():
            nothing(rows + 1)

    def time_taps(w, v):
        for a in range(3):
            outer = (w[a * 3].astype(jnp.float32) + w[a * 3 + 2].astype(jnp.float32)) * 0.5
            inner = w[a * 3 + 1].astype(jnp.float32) * 0.5
            v[a] = (outer - inner).astype(jnp.bfloat16)
            w[a * 3 + 1] = (outer + inner).astype(jnp.bfloat16)

    def frame(e):
        return xn[e].astype(jnp.float32)

    chunk = pix // 4
    col = lax.broadcasted_iota(jnp.int32, (chunk, chans), 0) % cols

    def product(w, v, k, e, at):
        total = None
        for a in range(3):
            tap = (w.at[a * 3], w.at[a * 3 + 1], v.at[a], w.at[a * 3 + 2])[k]
            part = jnp.dot(un[k, at + a * cols:at + a * cols + chunk, :], tap[:, e * chans:(e + 1) * chans],
                           preferred_element_type=jnp.float32)
            total = part if total is None else total + part
        return total

    def column(y, e):
        if e == 0:
            return jnp.where(col == 0, 0.0, pltpu.roll(y, 1, 0))
        if e == 2:
            return jnp.where(col == cols - 1, 0.0, pltpu.roll(y, chunk - 1, 0))
        return y

    def conv_late(w, v, f, bias):
        d1, d2, d3 = frame(f + 1), frame(f + 2), frame(f + 3)
        un[1] = (d1 + d2).astype(jnp.bfloat16)
        un[2] = (d2 - d1).astype(jnp.bfloat16)
        un[3] = (d1 - d3).astype(jnp.bfloat16)
        parts = []
        for at in range(0, pix, chunk):
            y0 = y1 = bias
            for e in (1, 0, 2):
                m1, m2, m3 = [product(w, v, k, e, at) for k in (1, 2, 3)]
                y0, y1 = y0 + column(m1 + m2, e), y1 + column(m1 - m2 - m3, e)
            acc[at:at + chunk] = y0
            parts.append(y1)
        return jnp.concatenate(parts, axis=0)

    def conv_early(w, v, f):
        un[0] = (frame(f) - frame(f + 2)).astype(jnp.bfloat16)
        parts = []
        for at in range(0, pix, chunk):
            y = acc[at:at + chunk]
            for e in (1, 0, 2):
                y = y + column(product(w, v, 0, e, at), e)
            parts.append(y)
        return jnp.concatenate(parts, axis=0)

    stats_start(0)
    halo_start(fx, 0, EDGES, 1)
    long_start(fx, 0, 0)
    halo_start(fx, 0, EDGES, 0)
    halo_start(fx, 0, MIDDLE, 1)
    halo_start(fx, 0, MIDDLE[:1], 0)
    for e in range(2, 2 + frames):
        halo_start(fx, 0, ROW, e)
    for c in small:
        c.wait()
    for c in taps[:3]:
        c.wait()
    time_taps(wa, va)

    def rest_first():
        for c in taps[3:]:
            c.wait()
        time_taps(wb, vb)
        long_start(fx, 0, 1)

    def edges_on(buf, n, e):
        halo_here(buf, n, EDGES, e)
        halo_edge(buf, n, e)

    stats_finish(0, par[0], par[1], rest_first)
    for e in range(2, 2 + frames):
        halo_here(fx, 0, ROW, e)
        normalise(fx, e)
    edges_on(fx, 0, 1)
    long_start(fx, 0, 2)

    def earlier(buf, n, i, e):
        @pl.when(i == 1)
        def _():
            halo_here(buf, n, MIDDLE, e)
            halo_corner(buf, n, e)
            normalise(buf, e)

    def first_conv(i, _):
        f = 2 - 2 * i

        def put(g, y):
            y = y.astype(jnp.bfloat16)
            bx[2 + g, 1:rows + 1] = y.reshape(rows, cols, chans)
            put_sums(1, g, *frame_sums(y.astype(jnp.float32)))
            halo_start(bx, 1, ROW, 2 + g)

        earlier(fx, 0, i, 1)
        put(f + 1, conv_late(wa, va, f, par[2]))

        @pl.when(i == 0)
        def _():
            long_start(bx, 1, 0)
            edges_on(fx, 0, 0)

        @pl.when(i == 1)
        def _():
            long_start(bx, 1, 1)

        earlier(fx, 0, i, 0)
        put(f, conv_early(wa, va, f))
        return 0

    lax.fori_loop(0, 2, first_conv, 0)

    stats_start(1)
    halo_start(bx, 1, EDGES, 1)
    halo_start(bx, 1, EDGES, 0)
    halo_start(bx, 1, MIDDLE[:1], 1)
    halo_start(bx, 1, MIDDLE, 0)
    stats_finish(1, par[3], par[4], lambda: long_start(bx, 1, 2))
    edges_on(bx, 1, 1)
    for e in range(2, 2 + frames):
        halo_here(bx, 1, ROW, e)
        normalise(bx, e)

    def second_conv(i, _):
        f = 2 - 2 * i

        def put(g, y):
            y = y + fx[2 + g, 1:rows + 1].reshape(pix, chans).astype(jnp.float32)
            out[g] = y.astype(jnp.bfloat16).reshape(rows, cols, chans)

        earlier(bx, 1, i, 1)
        put(f + 1, conv_late(wb, vb, f, par[5]))

        @pl.when(i == 0)
        def _():
            edges_on(bx, 1, 0)

        earlier(bx, 1, i, 0)
        put(f, conv_early(wb, vb, f))
        return 0

    lax.fori_loop(0, 2, second_conv, 0)

    for n, buf in enumerate((fx, bx)):
        for e in (1, 0):
            halo_sent(buf, n, [kind for kind in TIME if (kind, e) != LONG[n]], e)

            @pl.when(tm > 0)
            def _():
                halo_sent(buf, n, ROW, e)
        for e in range(2, 2 + frames):
            halo_sent(buf, n, ROW, e)
        stats_sent(n)
        long_sent(buf, n)


def solution(mesh):
    n_tm, n_rw = mesh.shape["tm"], mesh.shape["rows"]

    def on_device(features, gamma_one, beta_one, weight_one, bias_one, gamma_two, beta_two, weight_two, bias_two):
        frames, rows, cols, chans = features.shape
        taps = lambda w: w.reshape(9, 3, chans, chans)
        line = lambda v: v.reshape(1, chans)
        bf16, f32 = jnp.bfloat16, jnp.float32
        dma = pltpu.SemaphoreType.DMA
        return pl.pallas_call(
            functools.partial(block_kernel, n_tm, n_rw, frames, rows, cols, chans),
            out_shape=jax.ShapeDtypeStruct(features.shape, bf16),
            in_specs=[HBM] * 9,
            out_specs=pl.BlockSpec(memory_space=pltpu.VMEM),
            scratch_shapes=[
                pltpu.VMEM((frames + 2, rows + 2, cols, chans), bf16),
                pltpu.VMEM((frames + 2, rows + 2, cols, chans), bf16),
                pltpu.VMEM((frames + 2, (rows + 2) * cols, chans), bf16),
                pltpu.VMEM((4, (rows + 2) * cols, chans), bf16),
                pltpu.VMEM((rows * cols, chans), f32),
                pltpu.VMEM((9, chans, 3 * chans), bf16),
                pltpu.VMEM((9, chans, 3 * chans), bf16),
                pltpu.VMEM((3, chans, 3 * chans), bf16),
                pltpu.VMEM((3, chans, 3 * chans), bf16),
                pltpu.VMEM((6, 1, chans), f32),
                pltpu.VMEM((2, 2 * frames, chans), f32),
                pltpu.VMEM((2, 1, chans), f32),
                pltpu.VMEM((2, 3, 1, chans), f32),
                pltpu.VMEM((2, n_rw - 1, 3, 1, chans), f32),
                pltpu.VMEM((2, n_tm - 1, 1, chans), f32),
                pltpu.VMEM((3, 8, chans), f32),
                pltpu.VMEM((2, 2, rows // 4, cols, chans), bf16),
                dma((frames,)), dma((6,)), dma((2, 3)),
                dma((2,)), dma((2,)), dma((2,)), dma((2,)),
                dma((2, 6, frames + 2)), dma((2, 6, frames + 2)), dma((2, 3)), dma((2, 2)),
            ],
            compiler_params=pltpu.CompilerParams(
                collective_id=0, has_side_effects=True, vmem_limit_bytes=52 << 20),
        )(*[pltpu.with_memory_space_constraint(v, pltpu.HBM) for v in (
            features, line(gamma_one), line(beta_one), taps(weight_one), line(bias_one),
            line(gamma_two), line(beta_two), taps(weight_two), line(bias_two))])

    placed = (P("tm", "rows", None, None), P(), P(), P(), P(), P(), P(), P(), P())
    return jax.shard_map(on_device, mesh=mesh, in_specs=placed, out_specs=P("tm", "rows", None, None), check_vma=False)
```
